256 devices in a mesh: pb: 16 (over x_lo, z), ka: 8 (over y, core), ha: 2 (over x_hi).
Axes of the slice: x: 4 (x_hi: 2, x_lo: 2; x = x_hi * 2 + x_lo), y: 4, z: 8, core: 2. Of those that a mesh axis runs over, the one named last changes fastest.
Arguments:
- queries: bfloat16 [16384, 4096], P('pb', 'ha'), may hold values from -512 to 512
- keys: bfloat16 [16, 8, 128, 512], P('pb', 'ka', None, 'ha'), may hold values from -6 to 6
- values: bfloat16 [16, 8, 128, 512], P('pb', 'ka', None, 'ha'), may hold values from -6 to 6
- q_order: int32 [128], P('pb'), may hold values from 0 to 127, as said below
- block_mask: int32 [128, 128], P('pb'), may hold values from 0 to 1, as said below
Outputs:
- attended: bfloat16 [16384, 4096], P(('pb', 'ka'), 'ha')
The draws below stay inside these ranges and needn't reach their ends.
Inputs may be any that keep to these rules, and one draw needn't show every extreme that they name: `q_order`: slots 2m and 2m+1 hold query blocks i and 127 - i for some i, in either order; every block sits in exactly one slot. block_mask[s, b] is 1 only where b <= q_order[s], and block_mask[s, q_order[s]] is 1. For every m and every r below 8, slots 2m and 2m+1 together list at most 8 key blocks b with b % 8 == r, and exactly 8 for some m and r in every draw.
All inputs are finite; a program needn't handle non-finite values.
Results may differ from the reference program's by a relative error of at most 0.0042.
Values may be sent and summed in bfloat16 or wider, within the bound.
A program may use at most 128 MiB of HBM per device.

```python
import math
import jax
import jax.numpy as jnp
from jax import lax

HEAD_DIM = 128
Q_HEADS = 32
KV_HEADS = 4
BLOCK = 128
NBLOCKS = 128
TOKENS = 16384
RESIDUES = 8
PAIR_CAP = 8


def pairing_order(key):
    base = jax.random.fold_in(key, 101)
    half_count = NBLOCKS // 2
    early = jax.random.permutation(jax.random.fold_in(base, 1), half_count).astype(jnp.int32)
    flipped = jax.random.randint(jax.random.fold_in(base, 2), (half_count,), 0, 2)
    late = NBLOCKS - 1 - early
    first = jnp.where(flipped == 0, early, late)
    second = jnp.where(flipped == 0, late, early)
    return jnp.stack([first, second], axis=1).reshape(NBLOCKS).astype(jnp.int32)


def listed_blocks(key):
    order = pairing_order(key)
    base = jax.random.fold_in(key, 202)
    half_count = NBLOCKS // 2
    class_blocks = NBLOCKS // RESIDUES
    pair_blocks = order.reshape(half_count, 2)
    rows_t = jnp.arange(class_blocks, dtype=jnp.int32)
    rows_r = jnp.arange(RESIDUES, dtype=jnp.int32)
    block_ids = rows_t[:, None] * RESIDUES + rows_r[None, :]
    target = pair_blocks[:, :, None, None]
    usable = block_ids[None, None] <= target
    diagonal = block_ids[None, None] == target
    noise = jax.random.randint(jax.random.fold_in(base, 1), (half_count, 2, class_blocks, RESIDUES), 0, 2 ** 20)
    priority = jnp.where(diagonal, 2 ** 21, jnp.where(usable, noise, -1)).astype(jnp.int32)
    span_size = 2 * class_blocks
    grouped = jnp.transpose(priority, (0, 3, 1, 2)).reshape(half_count, RESIDUES, span_size)
    distinct = grouped * span_size + jnp.arange(span_size, dtype=jnp.int32)
    ranking = jnp.argsort(-distinct, axis=-1)
    placing = jnp.argsort(ranking, axis=-1)
    wanted = jax.random.randint(jax.random.fold_in(base, 2), (half_count, RESIDUES), PAIR_CAP // 2, PAIR_CAP + 1)
    forced = jax.random.randint(jax.random.fold_in(base, 3), (), 0, half_count * RESIDUES)
    flat_ids = jnp.arange(half_count * RESIDUES, dtype=jnp.int32).reshape(half_count, RESIDUES)
    wanted = jnp.where(flat_ids == forced, PAIR_CAP, wanted)
    chosen = placing < wanted[:, :, None]
    chosen = chosen.reshape(half_count, RESIDUES, 2, class_blocks).transpose(0, 2, 3, 1)
    return chosen.reshape(NBLOCKS, NBLOCKS).astype(jnp.int32)


def key_field(key):
    base = jax.random.fold_in(key, 303)
    shape = (NBLOCKS, BLOCK, KV_HEADS, HEAD_DIM)
    field = jnp.clip(jax.random.normal(jax.random.fold_in(base, 1), shape, jnp.float32), -6.0, 6.0)
    return field


def draw_queries(key, part):
    base = jax.random.fold_in(key, 404)
    shape = (NBLOCKS, BLOCK, KV_HEADS, Q_HEADS // KV_HEADS, HEAD_DIM)
    field = jnp.clip(jax.random.normal(jax.random.fold_in(base, 1), shape, jnp.float32), -6.0, 6.0)
    return field.reshape(NBLOCKS * BLOCK, Q_HEADS * HEAD_DIM).astype(jnp.bfloat16)


def draw_keys(key, part):
    field = key_field(key)
    return field.reshape(NBLOCKS // RESIDUES, RESIDUES, BLOCK, KV_HEADS * HEAD_DIM).astype(jnp.bfloat16)


def draw_q_order(key, part):
    return pairing_order(key)


def draw_block_mask(key, part):
    return listed_blocks(key)


def steps_of(rng, shape, shards, smallest, largest):
    loudness, own = 1.0, jax.random.fold_in(rng, 6)
    for dim, blocks in shards:
        steps = jnp.exp(jax.random.uniform(jax.random.fold_in(own, dim), (blocks,), jnp.float32, smallest / len(shards), largest / len(shards)))
        loudness = loudness * jnp.repeat(steps, shape[dim] // blocks).reshape([-1 if axis == dim else 1 for axis in range(len(shape))])
    return loudness


def normal_values(key, dims, spread, reach, cuts=(), kind=jnp.bfloat16):
    factor_of = steps_of(key, dims, cuts, -0.22, 0.18) if cuts else 1.0
    result = jax.random.normal(key, dims, jnp.float32) * spread * factor_of
    return jnp.minimum(jnp.maximum(result, -reach), reach).astype(kind)


def setup_inputs(seed: int = 0) -> dict:
    seeds = jax.random.split(jax.random.key(seed), 6)
    queries = draw_queries(jax.random.fold_in(seeds[5], 71), 0)
    keys = draw_keys(jax.random.fold_in(seeds[5], 71), 0)
    values = normal_values(seeds[2], (NBLOCKS // RESIDUES, RESIDUES, BLOCK, KV_HEADS * HEAD_DIM), 1.0, 6.0, ((0, 16), (1, 8), (3, 2)))
    q_order = draw_q_order(jax.random.fold_in(seeds[5], 71), 0)
    block_mask = draw_block_mask(jax.random.fold_in(seeds[5], 71), 0)
    return {"queries": queries, "keys": keys, "values": values, "q_order": q_order, "block_mask": block_mask}


masked_score = -1e+30

def compact(listed, entry_count):
    running = jnp.cumsum(listed, axis=1)
    span_size = listed.shape[1]
    ranks = jnp.arange(entry_count, dtype=jnp.int32)
    picked = (listed[:, None, :] == 1) & (running[:, None, :] == ranks[None, :, None] + 1)
    places = jnp.arange(span_size, dtype=jnp.int32)
    position = lax.optimization_barrier(jnp.sum(jnp.where(picked, places[None, None, :], 0), axis=2)).astype(jnp.int32)
    living = jnp.any(picked, axis=2)
    return (position, living)

def reference(queries, keys, values, q_order, block_mask):
    head_width = HEAD_DIM
    group_size = Q_HEADS // KV_HEADS
    key_pool = keys.reshape(NBLOCKS, BLOCK, KV_HEADS, head_width).astype(jnp.float32)
    value_pool = values.reshape(NBLOCKS, BLOCK, KV_HEADS, head_width).astype(jnp.float32)
    query_units = queries.reshape(NBLOCKS // 2, 2, BLOCK, KV_HEADS, group_size, head_width)
    listed = block_mask.reshape(NBLOCKS // 2, 2 * NBLOCKS)
    pair_blocks = q_order.reshape(NBLOCKS // 2, 2)
    entry_count = PAIR_CAP * RESIDUES
    causal = jnp.arange(BLOCK)[:, None] >= jnp.arange(BLOCK)[None, :]

    def one_pair(unit_args):
        query_unit, flags, query_blocks = unit_args
        position, living = compact(flags[None, :], entry_count)
        position = position[0]
        living = living[0]
        owners = position // NBLOCKS
        key_block = position % NBLOCKS
        query_rows = jnp.take(query_unit.astype(jnp.float32), owners, axis=0)
        key_rows = jnp.take(key_pool, key_block, axis=0)
        value_rows = jnp.take(value_pool, key_block, axis=0)
        scores = jnp.einsum('eigxd,ejgd->egxij', query_rows, key_rows, precision=lax.Precision.HIGHEST)
        scores = scores * (1.0 / math.sqrt(head_width))
        diagonal = key_block == jnp.take(query_blocks, owners, axis=0)
        allowed = living[:, None, None, None, None] & (jnp.logical_not(diagonal)[:, None, None, None, None] | causal[None, None, None])
        scores = jnp.where(allowed, scores, masked_score)
        row_peak = lax.optimization_barrier(jnp.max(scores, axis=4))
        belongs = owners[:, None] == jnp.arange(2)[None, :]
        slot_peak = lax.optimization_barrier(jnp.max(jnp.where(belongs[:, :, None, None, None], row_peak[:, None], masked_score), axis=0))
        top_rows = jnp.take(slot_peak, owners, axis=0)
        weights = jnp.where(allowed, jnp.exp(scores - top_rows[..., None]), 0.0)
        rounded = lax.optimization_barrier(weights.astype(jnp.bfloat16)).astype(jnp.float32)
        partial_sum = jnp.einsum('egxij,ejgd->eigxd', rounded, value_rows, precision=lax.Precision.HIGHEST)
        belongs_f = belongs.astype(jnp.float32)
        numerator = jnp.einsum('es,eigxd->sigxd', belongs_f, partial_sum, precision=lax.Precision.HIGHEST)
        denominator = jnp.einsum('es,egxij->sigx', belongs_f, weights, precision=lax.Precision.HIGHEST)
        attended = numerator / denominator[..., None]
        return attended.astype(jnp.bfloat16).reshape(2 * BLOCK, Q_HEADS * head_width)
    outputs = lax.map(one_pair, (query_units, listed, pair_blocks))
    return outputs.reshape(TOKENS, Q_HEADS * head_width)
```

```python
import functools
import math

import jax
import jax.numpy as jnp
from jax import lax
from jax.experimental import pallas as pl
from jax.experimental.pallas import tpu as pltpu
from jax.sharding import PartitionSpec as P

MESH = pl.DeviceIdType.MESH
BF16, F32, I32 = jnp.bfloat16, jnp.float32, jnp.int32
D = 128
GROUP = 8
LANES = GROUP * D
RING = 8
POOL = 64
NG = 17
SCALE = math.log2(math.e) / math.sqrt(D)
LOW = -1e30
VMEM_LIMIT = 60 * 1024 * 1024


def head_of(y):
    return lax.rem(lax.div(y + 1, 2), 2)


def gather_kernel(k_ref, v_ref, kbuf, vbuf, send, recv, local):
    pb, ka = lax.axis_index("pb"), lax.axis_index("ka")
    x, z = lax.div(pb, RING), lax.rem(pb, RING)
    y, c = lax.div(ka, 2), lax.rem(ka, 2)
    u = lax.rem(y, 2)
    mate = {"ka": (y + 1 - 2 * u) * 2 + c}
    across = {"pb": (1 - x) * RING + z}
    up = {"pb": x * RING + lax.rem(z + 1, RING)}
    down = {"pb": x * RING + lax.rem(z + RING - 1, RING)}
    sibling = {"ka": y * 2 + 1 - c}
    head = head_of(y)

    barrier = pltpu.get_barrier_semaphore()
    for who in (mate, across, up, down, sibling):
        pl.semaphore_signal(barrier, inc=1, device_id=who, device_id_type=MESH)
    pl.semaphore_wait(barrier, 5)

    started = []
    number = [0]

    def next_id():
        number[0] += 1
        return number[0] - 1

    def move(src, dst, landed, who):
        n = next_id()
        copy = pltpu.make_async_remote_copy(
            src_ref=src, dst_ref=dst, send_sem=send.at[n], recv_sem=recv.at[n],
            device_id=who, device_id_type=MESH,
        )
        copy.start()
        started.append(copy)
        return pltpu.make_async_remote_copy(
            src_ref=src, dst_ref=landed, send_sem=send.at[n], recv_sem=recv.at[n],
            device_id=who, device_id_type=MESH,
        )

    def ring(s):
        return lax.rem(z + s + RING, RING)

    def spot(core, zz, xx):
        return ((core * RING + zz) * 2 + xx) * 2

    base = spot(c, z, x)
    mine = [
        pltpu.make_async_copy(r.at[:, pl.ds(pl.multiple_of(head * D, D), D)], b.at[base + u], local.at[i])
        for i, (r, b) in enumerate(((k_ref, kbuf), (v_ref, vbuf)))
    ]
    for copy in mine:
        copy.start()
    other = pl.ds(pl.multiple_of((1 - head) * D, D), D)
    k_swap = move(k_ref.at[:, other], kbuf.at[base + u], kbuf.at[base + 1 - u], mate)
    v_swap = move(v_ref.at[:, other], vbuf.at[base + u], vbuf.at[base + 1 - u], mate)
    for copy in mine:
        copy.wait()

    late = []

    def blocks(buf, at, count):
        return buf.at[pl.ds(at, count)]

    def same(buf, at, count, who, landed):
        return move(blocks(buf, at, count), blocks(buf, at, count), blocks(buf, landed, count), who)

    def to_sibling(buf, core_spot, count):
        landed = core_spot + (1 - 2 * c) * (POOL // 2)
        late.append(same(buf, core_spot, count, sibling, landed))

    k_swap.wait_recv()
    k_cross = same(kbuf, base, 2, across, spot(c, z, 1 - x))
    v_swap.wait_recv()
    v_up = same(vbuf, base, 2, up, spot(c, ring(-1), x))
    v_down = same(vbuf, base, 2, down, spot(c, ring(1), x))
    v_cross = [same(vbuf, base, 2, across, spot(c, z, 1 - x))]
    crossed = [spot(c, z, 1 - x)]
    to_sibling(vbuf, base, 2)
    k_cross.wait_recv()
    k_up = same(kbuf, spot(c, z, 0), 4, up, spot(c, ring(-1), 0))
    k_down = same(kbuf, spot(c, z, 0), 4, down, spot(c, ring(1), 0))
    to_sibling(kbuf, spot(c, z, 0), 4)

    def forward_v(zz):
        v_cross.append(same(vbuf, spot(c, zz, x), 2, across, spot(c, zz, 1 - x)))
        crossed.append(spot(c, zz, 1 - x))
        to_sibling(vbuf, spot(c, zz, x), 2)

    for s in (1, 2, 3):
        lo, hi = ring(-s), ring(s)
        v_up.wait_recv()
        if s < 3:
            v_up = same(vbuf, spot(c, lo, x), 2, up, spot(c, ring(-s - 1), x))
        else:
            v_up = same(vbuf, spot(c, lo, x), 1, up, spot(c, ring(4), x))
        forward_v(lo)
        v_down.wait_recv()
        if s < 3:
            v_down = same(vbuf, spot(c, hi, x), 2, down, spot(c, ring(s + 1), x))
        else:
            v_down = same(vbuf, spot(c, hi, x) + 1, 1, down, spot(c, ring(4), x) + 1)
        forward_v(hi)
        k_up.wait_recv()
        if s < 3:
            k_up = same(kbuf, spot(c, lo, 0), 4, up, spot(c, ring(-s - 1), 0))
        else:
            k_up = same(kbuf, spot(c, lo, 0), 2, up, spot(c, ring(4), 0))
        to_sibling(kbuf, spot(c, lo, 0), 4)
        k_down.wait_recv()
        if s < 3:
            k_down = same(kbuf, spot(c, hi, 0), 4, down, spot(c, ring(s + 1), 0))
        else:
            k_down = same(kbuf, spot(c, hi, 1), 2, down, spot(c, ring(4), 1))
        to_sibling(kbuf, spot(c, hi, 0), 4)
        done = 1 if s == 1 else 2
        for _ in range(done):
            v_cross.pop(0).wait_recv()
            to_sibling(vbuf, crossed.pop(0), 2)
    far = ring(4)
    v_up.wait_recv()
    v_down.wait_recv()
    forward_v(far)
    k_up.wait_recv()
    k_down.wait_recv()
    to_sibling(kbuf, spot(c, far, 0), 4)
    while v_cross:
        v_cross.pop(0).wait_recv()
        to_sibling(vbuf, crossed.pop(0), 2)
    for copy in late:
        copy.wait_recv()
    for copy in started:
        copy.wait_send()


COPIES = 64


def gathered(keys, values):
    shape = jax.ShapeDtypeStruct((POOL, D, D), BF16)
    vmem = pl.BlockSpec(memory_space=pltpu.VMEM)
    return pl.pallas_call(
        gather_kernel,
        out_shape=(shape, shape),
        in_specs=[vmem, vmem],
        out_specs=(vmem, vmem),
        scratch_shapes=[
            pltpu.SemaphoreType.DMA((COPIES,)),
            pltpu.SemaphoreType.DMA((COPIES,)),
            pltpu.SemaphoreType.DMA((2,)),
        ],
        compiler_params=pltpu.CompilerParams(collective_id=0, has_side_effects=True),
        name="gather_blocks",
    )(keys, values)


def attend_kernel(nw, lst, ga, q_ref, k_ref, v_ref, o_ref, st_ref, qs, bias, acc, mb, lb):
    row = lax.broadcasted_iota(I32, (D, D), 0)
    col = lax.broadcasted_iota(I32, (D, D), 1)
    bias[0] = jnp.zeros((D, D), F32)
    bias[1] = jnp.where(row <= col, 0.0, LOW)
    bias[2] = jnp.full((D, D), LOW, F32)
    for s in range(4):
        for i in range(GROUP):
            qs[s, i * D:(i + 1) * D, :] = q_ref[s * D:(s + 1) * D, i * D:(i + 1) * D]
    for p in range(2):
        acc[0] = jnp.zeros((D, LANES), F32)
        mb[0] = jnp.full((8, LANES), LOW, F32)
        lb[0] = jnp.zeros((8, LANES), F32)
        first_groups = ga[p]

        def step(g, _):
            e0, e1 = lst[p, 2 * g], lst[p, 2 * g + 1]
            owner = (g >= first_groups).astype(I32)
            first = jnp.logical_or(g == 0, g == first_groups)
            i0, i1 = e0 & (POOL - 1), e1 & (POOL - 1)
            k = jnp.concatenate([k_ref[i0], k_ref[i1]], axis=0)
            v = jnp.concatenate([v_ref[i0], v_ref[i1]], axis=0)
            b = jnp.concatenate([bias[e0 >> 6], bias[e1 >> 6]], axis=0)
            vt = v.T
            for w in range(0, LANES, nw):
                q = qs[2 * p + owner, w:w + nw, :]
                s = lax.dot_general(k, q, (((1,), (1,)), ((), ())), preferred_element_type=F32)
                s = s + jnp.concatenate([b] * (nw // D), axis=1)
                old = jnp.where(first, -3e38, mb[g, 0:1, w:w + nw])
                m = jnp.maximum(old, jnp.max(s, axis=0, keepdims=True))
                alpha = jnp.exp2((old - m) * SCALE)
                weights = jnp.exp2((s - m) * SCALE)
                l = lb[g, 0:1, w:w + nw] * alpha + jnp.sum(weights, axis=0, keepdims=True)
                pv = lax.dot_general(
                    vt, weights.astype(BF16), (((1,), (0,)), ((), ())), preferred_element_type=F32
                )
                acc[g + 1, :, w:w + nw] = acc[g, :, w:w + nw] * alpha + pv
                mb[g + 1, 0:1, w:w + nw] = m
                lb[g + 1, 0:1, w:w + nw] = l
            return 0

        lax.fori_loop(0, NG, step, 0)
        for j in range(2):
            at = first_groups if j == 0 else NG
            o_ref[2 * p + j] = acc[at].astype(BF16)
            st_ref[2 * p + j, 0:1] = mb[at, 0:1]
            st_ref[2 * p + j, 1:2] = lb[at, 0:1]


def attended_parts(listing, first_groups, q, k, v):
    vmem = pl.BlockSpec(memory_space=pltpu.VMEM)
    smem = pl.BlockSpec(memory_space=pltpu.SMEM)
    return pl.pallas_call(
        functools.partial(attend_kernel, 128),
        out_shape=(
            jax.ShapeDtypeStruct((4, D, LANES), BF16),
            jax.ShapeDtypeStruct((4, 8, LANES), F32),
        ),
        in_specs=[smem, smem, vmem, vmem, vmem],
        out_specs=(vmem, vmem),
        scratch_shapes=[
            pltpu.VMEM((4, LANES, D), BF16),
            pltpu.VMEM((3, D, D), F32),
            pltpu.VMEM((NG + 1, D, LANES), F32),
            pltpu.VMEM((NG + 1, 8, LANES), F32),
            pltpu.VMEM((NG + 1, 8, LANES), F32),
        ],
        compiler_params=pltpu.CompilerParams(vmem_limit_bytes=VMEM_LIMIT),
        name="attend",
    )(listing, first_groups, q, k, v)


def merge_kernel(o_ref, st_ref, out_ref, ro, rs, send, recv, local):
    ka = lax.axis_index("ka")
    y, c = lax.div(ka, 2), lax.rem(ka, 2)
    barrier = pltpu.get_barrier_semaphore()
    for d in range(1, 8):
        pl.semaphore_signal(barrier, inc=1, device_id={"ka": lax.rem(ka + d, 8)}, device_id_type=MESH)
    pl.semaphore_wait(barrier, 7)

    def remote(src, dst, n, m, who):
        return pltpu.make_async_remote_copy(
            src_ref=src, dst_ref=dst, send_sem=send.at[n], recv_sem=recv.at[m],
            device_id=who, device_id_type=MESH,
        )

    parts = []
    for i in range(4):
        target = (2 * c + i // 2) * 2 + i % 2
        here = target == ka
        away = jnp.logical_not(here)
        for kind, (src, dst) in enumerate(((o_ref, ro), (st_ref, rs))):
            far = remote(src.at[i], dst.at[y], 2 * i + kind, 2 * y + kind, {"ka": target})
            near = pltpu.make_async_copy(src.at[i], dst.at[y], local.at[kind])
            pl.when(away)(far.start)
            pl.when(here)(near.start)
            parts.append((here, away, far, near))
    for yy in range(4):
        own = jnp.logical_and(yy == y, c == lax.div(y, 2))
        for kind, (src, dst) in enumerate(((o_ref, ro), (st_ref, rs))):
            come = remote(src.at[0], dst.at[yy], kind, 2 * yy + kind, {"ka": lax.rem(ka + 1, 8)})
            pl.when(jnp.logical_not(own))(come.wait_recv)
    for here, away, far, near in parts:
        pl.when(here)(near.wait)
    for head, (a, b) in enumerate(((0, 3), (1, 2))):
        ma, mb = rs[a, 0:1], rs[b, 0:1]
        top = jnp.maximum(ma, mb)
        fa, fb = jnp.exp2((ma - top) * SCALE), jnp.exp2((mb - top) * SCALE)
        whole = fa * rs[a, 1:2] + fb * rs[b, 1:2]
        fa, fb = fa / whole, fb / whole
        for i in range(GROUP):
            cut = slice(i * D, (i + 1) * D)
            both = ro[a, :, cut].astype(F32) * fa[:, cut] + ro[b, :, cut].astype(F32) * fb[:, cut]
            at = head * LANES + i * D
            out_ref[:, at:at + D] = both.T.astype(BF16)
    for here, away, far, near in parts:
        pl.when(away)(far.wait_send)


def merged(o, st):
    vmem = pl.BlockSpec(memory_space=pltpu.VMEM)
    return pl.pallas_call(
        merge_kernel,
        out_shape=jax.ShapeDtypeStruct((D, 2 * LANES), BF16),
        in_specs=[vmem, vmem],
        out_specs=vmem,
        scratch_shapes=[
            pltpu.VMEM((4, D, LANES), BF16),
            pltpu.VMEM((4, 8, LANES), F32),
            pltpu.SemaphoreType.DMA((8,)),
            pltpu.SemaphoreType.DMA((8,)),
            pltpu.SemaphoreType.DMA((2,)),
        ],
        compiler_params=pltpu.CompilerParams(collective_id=1, has_side_effects=True),
        name="merge_parts",
    )(o, st)


def in_pool_order(x):
    x = x.reshape(*x.shape[:-1], 2, RING, 2, 2, 2)
    return x


def listing_of(q_order, block_mask, group, core):
    mask = lax.dynamic_slice_in_dim(block_mask, 4 * core, 4, 0).reshape(4, 2, RING, 2, 2, 2)
    order = lax.dynamic_slice_in_dim(q_order, 4 * core, 4, 0)
    mask = lax.dynamic_index_in_dim(mask, group, 3, keepdims=False)
    ids = jnp.arange(2 * POOL, dtype=I32).reshape(2, RING, 2, 2, 2)
    ids = lax.dynamic_index_in_dim(ids, group, 2, keepdims=False)
    mask = mask.transpose(0, 4, 2, 1, 3).reshape(2, 2, POOL)
    ids = ids.transpose(3, 1, 0, 2).reshape(POOL)
    diagonal = (ids[None, None, :] == order.reshape(2, 2, 1)).astype(I32)
    value = jnp.arange(POOL, dtype=I32) + POOL * diagonal
    upto = (jnp.arange(POOL)[:, None] <= jnp.arange(POOL)[None, :]).astype(F32)
    rank = jnp.einsum("pjb,bc->pjc", mask.astype(F32), upto).astype(I32)
    total = rank[:, 0, -1]
    first_groups = jnp.maximum((total + 1) // 2, 1)
    start = jnp.stack([jnp.zeros_like(first_groups), 2 * first_groups], axis=1)
    at = rank - 1 + start[:, :, None]
    hit = (mask[..., None] == 1) & (at[..., None] == jnp.arange(2 * NG, dtype=I32))
    listing = 2 * POOL + jnp.sum(jnp.where(hit, value[..., None] - 2 * POOL, 0), axis=(1, 2))
    return listing.astype(I32), first_groups.astype(I32)


def on_device(queries, keys, values, q_order, block_mask):
    ka = lax.axis_index("ka")
    y, c = ka // 2, ka % 2
    listing, first_groups = listing_of(q_order, block_mask, y // 2, c)
    k, v = gathered(keys.reshape(D, 2 * D), values.reshape(D, 2 * D))
    q = lax.dynamic_slice(queries, (4 * D * c, LANES * head_of(y)), (4 * D, LANES))
    o, st = attended_parts(listing, first_groups, q, k, v)
    return merged(o, st)


def solution(mesh):
    in_specs = (P("pb", "ha"), P("pb", "ka", None, "ha"), P("pb", "ka", None, "ha"), P("pb"), P("pb", None))
    return jax.shard_map(
        on_device, mesh=mesh, in_specs=in_specs, out_specs=P(("pb", "ka"), "ha"), check_vma=False
    )
```

```python
import functools
import math

import jax
import jax.numpy as jnp
from jax import lax
from jax.experimental import pallas as pl
from jax.experimental.pallas import tpu as pltpu
from jax.sharding import PartitionSpec as P

MESH = pl.DeviceIdType.MESH
BF16, F32, I32 = jnp.bfloat16, jnp.float32, jnp.int32
D = 128
GROUP = 8
LANES = GROUP * D
RING = 8
POOL = 64
NG = 17
SCALE = math.log2(math.e) / math.sqrt(D)
LOW = -1e30
VMEM_LIMIT = 60 * 1024 * 1024


def head_of(y):
    return lax.rem(lax.div(y + 1, 2), 2)


def gather(k_ref, v_ref, kbuf, vbuf, send, recv, local, meanwhile):
    pb, ka = lax.axis_index("pb"), lax.axis_index("ka")
    x, z = lax.div(pb, RING), lax.rem(pb, RING)
    y, c = lax.div(ka, 2), lax.rem(ka, 2)
    u = lax.rem(y, 2)
    mate = {"ka": (y + 1 - 2 * u) * 2 + c}
    across = {"pb": (1 - x) * RING + z}
    up = {"pb": x * RING + lax.rem(z + 1, RING)}
    down = {"pb": x * RING + lax.rem(z + RING - 1, RING)}
    sibling = {"ka": y * 2 + 1 - c}
    head = head_of(y)

    started = []
    number = [0]

    def next_id():
        number[0] += 1
        return number[0] - 1

    def move(src, dst, landed, who):
        n = next_id()
        copy = pltpu.make_async_remote_copy(
            src_ref=src, dst_ref=dst, send_sem=send.at[n], recv_sem=recv.at[n],
            device_id=who, device_id_type=MESH,
        )
        copy.start()
        started.append(copy)
        return pltpu.make_async_remote_copy(
            src_ref=src, dst_ref=landed, send_sem=send.at[n], recv_sem=recv.at[n],
            device_id=who, device_id_type=MESH,
        )

    def ring(s):
        return lax.rem(z + s + RING, RING)

    def spot(core, zz, xx):
        return ((core * RING + zz) * 2 + xx) * 2

    base = spot(c, z, x)
    mine = [
        pltpu.make_async_copy(r.at[:, pl.ds(pl.multiple_of(head * D, D), D)], b.at[base + u], local.at[i])
        for i, (r, b) in enumerate(((k_ref, kbuf), (v_ref, vbuf)))
    ]
    for copy in mine:
        copy.start()
    other = pl.ds(pl.multiple_of((1 - head) * D, D), D)
    k_swap = move(k_ref.at[:, other], kbuf.at[base + u], kbuf.at[base + 1 - u], mate)
    v_swap = move(v_ref.at[:, other], vbuf.at[base + u], vbuf.at[base + 1 - u], mate)
    meanwhile()
    for copy in mine:
        copy.wait()

    late = []

    def blocks(buf, at, count):
        return buf.at[pl.ds(at, count)]

    def same(buf, at, count, who, landed):
        return move(blocks(buf, at, count), blocks(buf, at, count), blocks(buf, landed, count), who)

    def to_sibling(buf, core_spot, count):
        landed = core_spot + (1 - 2 * c) * (POOL // 2)
        late.append(same(buf, core_spot, count, sibling, landed))

    k_swap.wait_recv()
    k_cross = same(kbuf, base, 2, across, spot(c, z, 1 - x))
    v_swap.wait_recv()
    v_up = same(vbuf, base, 2, up, spot(c, ring(-1), x))
    v_down = same(vbuf, base, 2, down, spot(c, ring(1), x))
    v_cross = [same(vbuf, base, 2, across, spot(c, z, 1 - x))]
    crossed = [spot(c, z, 1 - x)]
    to_sibling(vbuf, base, 2)
    k_cross.wait_recv()
    k_up = same(kbuf, spot(c, z, 0), 4, up, spot(c, ring(-1), 0))
    k_down = same(kbuf, spot(c, z, 0), 4, down, spot(c, ring(1), 0))
    to_sibling(kbuf, spot(c, z, 0), 4)

    def forward_v(zz):
        v_cross.append(same(vbuf, spot(c, zz, x), 2, across, spot(c, zz, 1 - x)))
        crossed.append(spot(c, zz, 1 - x))
        to_sibling(vbuf, spot(c, zz, x), 2)

    for s in (1, 2, 3):
        lo, hi = ring(-s), ring(s)
        v_up.wait_recv()
        if s < 3:
            v_up = same(vbuf, spot(c, lo, x), 2, up, spot(c, ring(-s - 1), x))
        else:
            v_up = same(vbuf, spot(c, lo, x), 1, up, spot(c, ring(4), x))
        forward_v(lo)
        v_down.wait_recv()
        if s < 3:
            v_down = same(vbuf, spot(c, hi, x), 2, down, spot(c, ring(s + 1), x))
        else:
            v_down = same(vbuf, spot(c, hi, x) + 1, 1, down, spot(c, ring(4), x) + 1)
        forward_v(hi)
        k_up.wait_recv()
        if s < 3:
            k_up = same(kbuf, spot(c, lo, 0), 4, up, spot(c, ring(-s - 1), 0))
        else:
            k_up = same(kbuf, spot(c, lo, 0), 2, up, spot(c, ring(4), 0))
        to_sibling(kbuf, spot(c, lo, 0), 4)
        k_down.wait_recv()
        if s < 3:
            k_down = same(kbuf, spot(c, hi, 0), 4, down, spot(c, ring(s + 1), 0))
        else:
            k_down = same(kbuf, spot(c, hi, 1), 2, down, spot(c, ring(4), 1))
        to_sibling(kbuf, spot(c, hi, 0), 4)
        done = 1 if s == 1 else 2
        for _ in range(done):
            v_cross.pop(0).wait_recv()
            to_sibling(vbuf, crossed.pop(0), 2)
    far = ring(4)
    v_up.wait_recv()
    v_down.wait_recv()
    forward_v(far)
    k_up.wait_recv()
    k_down.wait_recv()
    to_sibling(kbuf, spot(c, far, 0), 4)
    while v_cross:
        v_cross.pop(0).wait_recv()
        to_sibling(vbuf, crossed.pop(0), 2)
    for copy in late:
        copy.wait_recv()
    for copy in started:
        copy.wait_send()


COPIES = 64


HALF = 512
CHUNK = 256
EXTRA = 16
UNROLL = 5


def fused_kernel(lst, ga, q_hbm, k_ref, v_ref, out_ref, kbuf, vbuf, qs, bias, acc, mb, sb, obuf, sbuf, land, lstat,
                 send, recv, local, qsem, xsend, xrecv, rsend, near_sem):
    pb, ka = lax.axis_index("pb"), lax.axis_index("ka")
    x, z = lax.div(pb, RING), lax.rem(pb, RING)
    y, c = lax.div(ka, 2), lax.rem(ka, 2)
    head = head_of(y)

    barrier = pltpu.get_barrier_semaphore()
    partners = [{"ka": lax.rem(ka + d, 8)} for d in range(1, 8)]
    partners += [
        {"pb": (1 - x) * RING + z},
        {"pb": x * RING + lax.rem(z + 1, RING)},
        {"pb": x * RING + lax.rem(z + RING - 1, RING)},
    ]
    for who in partners:
        pl.semaphore_signal(barrier, inc=1, device_id=who, device_id_type=MESH)
    pl.semaphore_wait(barrier, len(partners))

    fetch = []

    def meanwhile():
        for s in range(4):
            for i in range(GROUP):
                rows = pl.ds(pl.multiple_of((4 * c + s) * D, D), D)
                cols = pl.ds(pl.multiple_of(head * LANES + i * D, D), D)
                copy = pltpu.make_async_copy(
                    q_hbm.at[rows, cols], qs.at[s, pl.ds(i * D, D)], qsem.at[s * GROUP + i]
                )
                copy.start()
                fetch.append(copy)
        row = lax.broadcasted_iota(I32, (D, D), 0)
        col = lax.broadcasted_iota(I32, (D, D), 1)
        bias[0] = jnp.zeros((D, D), F32)
        bias[1] = jnp.where(row <= col, 0.0, LOW)
        acc[0] = jnp.zeros(acc.shape[1:], F32)
        mb[0] = jnp.full(mb.shape[1:], LOW, F32)

    gather(k_ref, v_ref, kbuf, vbuf, send, recv, local, meanwhile)
    for copy in fetch:
        copy.wait()

    ones = jnp.where(lax.broadcasted_iota(I32, (EXTRA, 2 * D), 0) == 0, 1.0, 0.0).astype(BF16)

    def entry(p, g):
        return lst[p, 2 * g], lst[p, 2 * g + 1]

    def scores(p, g, half, w):
        e0, e1 = entry(p, g)
        owner = (g >= ga[p]).astype(I32)
        k = jnp.concatenate([kbuf[e0 & (POOL - 1)], kbuf[e1 & (POOL - 1)]], axis=0)
        q = qs[2 * p + owner, half * HALF + w:half * HALF + w + CHUNK, :]
        return lax.dot_general(k, q, (((1,), (1,)), ((), ())), preferred_element_type=F32)

    def stage(p, g, half, diagonal, more=True):
        e0, e1 = entry(p, g)
        first = jnp.logical_or(g == 0, g == ga[p])
        pad0, pad1 = e0 >= 2 * POOL, e1 >= 2 * POOL
        v = jnp.concatenate([vbuf[e0 & (POOL - 1)], vbuf[e1 & (POOL - 1)]], axis=0)
        vt = jnp.concatenate([v.T, ones], axis=0)
        now, then = lax.rem(jnp.int32(g), 2), lax.rem(jnp.int32(g) + 1, 2)
        for w in range(0, HALF, CHUNK):
            cut = slice(w, w + CHUNK)
            s0, s1 = sb[now, 0:D, cut], sb[now, D:2 * D, cut]
            if more:
                sb[then, :, cut] = scores(p, g + 1, half, w)
            if diagonal == 0:
                s0 = s0 + jnp.concatenate([bias[(e0 >> 6) & 1]] * (CHUNK // D), axis=1)
            if diagonal == 1:
                s1 = s1 + jnp.concatenate([bias[(e1 >> 6) & 1]] * (CHUNK // D), axis=1)
            old = jnp.where(first, -3e38, mb[g, 0:1, cut])
            m0 = jnp.where(pad0, LOW, jnp.max(s0, axis=0, keepdims=True))
            m1 = jnp.where(pad1, LOW, jnp.max(s1, axis=0, keepdims=True))
            m = jnp.maximum(old, jnp.maximum(m0, m1))
            alpha = jnp.exp2((old - m) * SCALE)
            w0 = jnp.exp2((s0 - jnp.where(pad0, -LOW, m)) * SCALE).astype(BF16)
            w1 = jnp.exp2((s1 - jnp.where(pad1, -LOW, m)) * SCALE).astype(BF16)
            part = lax.dot_general(
                vt, jnp.concatenate([w0, w1], axis=0), (((1,), (0,)), ((), ())), preferred_element_type=F32
            )
            acc[g + 1, :, cut] = acc[g, :, cut] * alpha + part
            mb[g + 1, 0:1, cut] = m

    near = lax.div(y, 2) == c
    odd = lax.rem(y, 2)
    last = jnp.where(near, odd, 1 - odd)
    away = jnp.logical_not(near)
    pending = []

    def remote(src, dst, ssem, rsem, who):
        return pltpu.make_async_remote_copy(
            src_ref=src, dst_ref=dst, send_sem=ssem, recv_sem=rsem, device_id=who, device_id_type=MESH
        )

    kinds = ((obuf, land), (sbuf, lstat))
    relay_up = lax.div(lax.rem(y + 3, 4), 2) != c
    relay_from = jnp.where(relay_up, lax.rem(y + 3, 4), lax.rem(y + 1, 4))
    relay_to = jnp.where(relay_up, lax.rem(y + 1, 4), lax.rem(y + 3, 4)) * 2 + jnp.where(relay_up, 0, 1)

    def arrived(at, half, kind):
        dst = kinds[kind][1]
        return remote(dst.at[at, half], dst.at[at, half], xsend.at[0, 0, kind], xrecv.at[at, half, kind],
                      {"ka": lax.rem(ka + 1, 8)})

    def relay(half):
        for kind in range(2):
            arrived(4, half, kind).wait_recv()
            dst = kinds[kind][1]
            copy = remote(dst.at[4, half], dst.at[relay_from, half], rsend.at[half, kind],
                          xrecv.at[relay_from, half, kind], {"ka": relay_to})
            copy.start()
            pending.append((None, copy))

    for phase in range(4):
        half = phase % 2
        p = jnp.where(phase < 2, 1 - last, last)
        for w in range(0, HALF, CHUNK):
            sb[0, :, w:w + CHUNK] = scores(p, 0, half, w)
        stage(p, 0, half, 0)

        def step(i, _):
            for t in range(UNROLL):
                stage(p, 1 + i * UNROLL + t, half, None)
            return 0

        lax.fori_loop(0, (NG - 2) // UNROLL, step, 0)
        stage(p, NG - 1, half, 1, more=False)
        for j in range(2):
            at = ga[p] if j == 0 else NG
            obuf[2 * phase + j] = acc[at, 0:D].astype(BF16)
            sbuf[2 * phase + j, 0:1] = mb[at, 0:1]
            sbuf[2 * phase + j, 1:2] = acc[at, D:D + 1]
        for j in range(2):
            for kind, (src, dst) in enumerate(kinds):
                n = 2 * phase + j
                if phase < 2:
                    target = jnp.where(near, (y + 1 - 2 * odd) * 2 + j, lax.rem(y + (1 if j == 0 else 3), 4) * 2 + c)
                    spot = jnp.where(near, y, 4)
                    copy = remote(src.at[n], dst.at[spot, half], xsend.at[n, 0, kind], xrecv.at[spot, half, kind],
                                  {"ka": target})
                    copy.start()
                    pending.append((None, copy))
                else:
                    target = jnp.where(near, y, 3 - y) * 2 + j
                    mine = target == ka
                    copy = remote(src.at[n], dst.at[y, half], xsend.at[n, 0, kind], xrecv.at[y, half, kind],
                                  {"ka": target})
                    stay = pltpu.make_async_copy(src.at[n], dst.at[y, half], near_sem.at[half, kind])
                    pl.when(jnp.logical_not(mine))(copy.start)
                    pl.when(mine)(stay.start)
                    pending.append((jnp.logical_not(mine), copy))
        if phase == 1:
            relay(0)
        if phase == 2:
            relay(1)

    for half in range(2):
        for yy in range(4):
            here = jnp.logical_and(yy == y, near)
            for kind in range(2):
                pl.when(jnp.logical_not(here))(arrived(yy, half, kind).wait_recv)
                src, dst = kinds[kind]
                stay = pltpu.make_async_copy(src.at[0], dst.at[yy, half], near_sem.at[half, kind])
                pl.when(here)(stay.wait)
        for kv, (a, b) in enumerate(((0, 3), (1, 2))):
            ma, mb_ = lstat[a, half, 0:1], lstat[b, half, 0:1]
            top = jnp.maximum(ma, mb_)
            fa, fb = jnp.exp2((ma - top) * SCALE), jnp.exp2((mb_ - top) * SCALE)
            whole = fa * lstat[a, half, 1:2] + fb * lstat[b, half, 1:2]
            fa, fb = fa / whole, fb / whole
            for i in range(HALF // D):
                cut = slice(i * D, (i + 1) * D)
                both = land[a, half, :, cut].astype(F32) * fa[:, cut] + land[b, half, :, cut].astype(F32) * fb[:, cut]
                at = kv * LANES + half * HALF + i * D
                out_ref[:, at:at + D] = both.T.astype(BF16)
    for when, copy in pending:
        if when is None:
            copy.wait_send()
        else:
            pl.when(when)(copy.wait_send)


def fused(listing, first_groups, queries, keys, values):
    vmem = pl.BlockSpec(memory_space=pltpu.VMEM)
    smem = pl.BlockSpec(memory_space=pltpu.SMEM)
    dma = pltpu.SemaphoreType.DMA
    return pl.pallas_call(
        fused_kernel,
        out_shape=jax.ShapeDtypeStruct((D, 2 * LANES), BF16),
        in_specs=[smem, smem, pl.BlockSpec(memory_space=pl.ANY), vmem, vmem],
        out_specs=vmem,
        scratch_shapes=[
            pltpu.VMEM((POOL, D, D), BF16),
            pltpu.VMEM((POOL, D, D), BF16),
            pltpu.VMEM((4, LANES, D), BF16),
            pltpu.VMEM((2, D, D), F32),
            pltpu.VMEM((NG + 1, D + EXTRA, HALF), F32),
            pltpu.VMEM((NG + 1, 8, HALF), F32),
            pltpu.VMEM((2, 2 * D, HALF), F32),
            pltpu.VMEM((8, D, HALF), BF16),
            pltpu.VMEM((8, 8, HALF), F32),
            pltpu.VMEM((5, 2, D, HALF), BF16),
            pltpu.VMEM((5, 2, 8, HALF), F32),
            dma((COPIES,)), dma((COPIES,)), dma((2,)), dma((4 * GROUP,)),
            dma((8, 1, 2)), dma((5, 2, 2)), dma((2, 2)), dma((2, 2)),
        ],
        compiler_params=pltpu.CompilerParams(
            collective_id=0, has_side_effects=True, vmem_limit_bytes=VMEM_LIMIT,
        ),
        name="attend_all",
    )(listing, first_groups, queries, keys, values)


def listing_of(q_order, block_mask, group, core):
    mask = lax.dynamic_slice_in_dim(block_mask, 4 * core, 4, 0).reshape(4, 2, RING, 2, 2, 2)
    order = lax.dynamic_slice_in_dim(q_order, 4 * core, 4, 0)
    mask = lax.dynamic_index_in_dim(mask, group, 3, keepdims=False)
    ids = jnp.arange(2 * POOL, dtype=I32).reshape(2, RING, 2, 2, 2)
    ids = lax.dynamic_index_in_dim(ids, group, 2, keepdims=False)
    mask = mask.transpose(0, 4, 2, 1, 3).reshape(2, 2, POOL)
    ids = ids.transpose(3, 1, 0, 2).reshape(POOL)
    diagonal = (ids[None, None, :] == order.reshape(2, 2, 1)).astype(I32)
    value = jnp.arange(POOL, dtype=I32) + POOL * diagonal
    upto = (jnp.arange(POOL)[:, None] <= jnp.arange(POOL)[None, :]).astype(F32)
    rest = mask * (1 - diagonal)
    rank = jnp.einsum("pjb,bc->pjc", rest.astype(F32), upto).astype(I32)
    has = jnp.sum(mask * diagonal, axis=-1, keepdims=True)
    count = rank[:, 0, -1] + has[:, 0, 0]
    first_groups = jnp.maximum((count + 1) // 2, 1)
    front = jnp.where(diagonal == 1, 0, rank - 1 + has)[:, 0]
    back = jnp.where(diagonal == 1, 2 * NG - 1, 2 * NG - rank - has)[:, 1]
    at = jnp.stack([front, back], axis=1)
    hit = (mask[..., None] == 1) & (at[..., None] == jnp.arange(2 * NG, dtype=I32))
    listing = 2 * POOL + jnp.sum(jnp.where(hit, value[..., None] - 2 * POOL, 0), axis=(1, 2))
    return listing.astype(I32), first_groups.astype(I32)


def on_device(queries, keys, values, q_order, block_mask):
    ka = lax.axis_index("ka")
    listing, first_groups = listing_of(q_order, block_mask, ka // 4, ka % 2)
    return fused(listing, first_groups, queries, keys.reshape(D, 2 * D), values.reshape(D, 2 * D))


def solution(mesh):
    in_specs = (P("pb", "ha"), P("pb", "ka", None, "ha"), P("pb", "ka", None, "ha"), P("pb"), P("pb", None))
    return jax.shard_map(
        on_device, mesh=mesh, in_specs=in_specs, out_specs=P(("pb", "ka"), "ha"), check_vma=False
    )
```

```python
import functools
import math

import jax
import jax.numpy as jnp
from jax import lax
from jax.experimental import pallas as pl
from jax.experimental.pallas import tpu as pltpu
from jax.sharding import PartitionSpec as P

MESH = pl.DeviceIdType.MESH
K, V = 0, 1
BF16, F32, I32 = jnp.bfloat16, jnp.float32, jnp.int32
D = 128
GROUP = 8
LANES = GROUP * D
RING = 8
POOL = 64
NG = 9
WIDE = 4
SCALE = math.log2(math.e) / math.sqrt(D)
LOW = -1e30
VMEM_LIMIT = 60 * 1024 * 1024


def head_of(y):
    return lax.rem(lax.div(y + 1, 2), 2)


def gather(k_ref, v_ref, kbuf, vbuf, send, recv, local, meanwhile, later):
    pb, ka = lax.axis_index("pb"), lax.axis_index("ka")
    x, z = lax.div(pb, RING), lax.rem(pb, RING)
    y, c = lax.div(ka, 2), lax.rem(ka, 2)
    u = lax.rem(y, 2)
    mate = {"ka": (y + 1 - 2 * u) * 2 + c}
    across = {"pb": (1 - x) * RING + z}
    up = {"pb": x * RING + lax.rem(z + 1, RING)}
    down = {"pb": x * RING + lax.rem(z + RING - 1, RING)}
    sibling = {"ka": y * 2 + 1 - c}
    corner = {"pb": (1 - x) * RING + z, "ka": (y + 1 - 2 * u) * 2 + c}
    head = head_of(y)

    started = []
    number = [0]

    def next_id():
        number[0] += 1
        return number[0] - 1

    def move(src, dst, landed, who):
        n = next_id()
        copy = pltpu.make_async_remote_copy(
            src_ref=src, dst_ref=dst, send_sem=send.at[n], recv_sem=recv.at[n],
            device_id=who, device_id_type=MESH,
        )
        copy.start()
        started.append(copy)
        return pltpu.make_async_remote_copy(
            src_ref=src, dst_ref=landed, send_sem=send.at[n], recv_sem=recv.at[n],
            device_id=who, device_id_type=MESH,
        )

    def ring(s):
        return lax.rem(z + s + RING, RING)

    def spot(core, zz, uu, xx):
        return ((core * RING + zz) * 2 + uu) * 2 + xx

    late = []

    def blocks(buf, at, count):
        return buf.at[pl.ds(at, count)]

    def same(buf, at, count, who, landed):
        return move(blocks(buf, at, count), blocks(buf, at, count), blocks(buf, landed, count), who)

    def to_sibling(buf, at, count):
        late.append(same(buf, at, count, sibling, at + (1 - 2 * c) * (POOL // 2)))

    own_u, new_u = u, 1 - u
    own, new = spot(c, z, own_u, x), spot(c, z, new_u, x)
    ours = pl.ds(pl.multiple_of(head * D, D), D)
    theirs = pl.ds(pl.multiple_of((1 - head) * D, D), D)
    k_swap = move(k_ref.at[:, theirs], kbuf.at[own], kbuf.at[new], mate)
    v_swap = move(v_ref.at[:, theirs], vbuf.at[own], vbuf.at[new], mate)
    k_cross = move(k_ref.at[:, ours], kbuf.at[own], kbuf.at[spot(c, z, own_u, 1 - x)], across)
    k_diagonal = move(k_ref.at[:, theirs], kbuf.at[own], kbuf.at[spot(c, z, new_u, 1 - x)], corner)
    v_up = [move(v_ref.at[:, ours], vbuf.at[own], vbuf.at[spot(c, ring(-1), own_u, x)], up)]
    v_down = [move(v_ref.at[:, ours], vbuf.at[own], vbuf.at[spot(c, ring(1), own_u, x)], down)]
    v_cross = [(z, own_u, move(v_ref.at[:, ours], vbuf.at[own], vbuf.at[spot(c, z, own_u, 1 - x)], across))]
    mine = [
        pltpu.make_async_copy(r.at[:, ours], b.at[own], local.at[i])
        for i, (r, b) in enumerate(((k_ref, kbuf), (v_ref, vbuf)))
    ]
    for copy in mine:
        copy.start()
    meanwhile()
    for copy in mine:
        copy.wait()

    def cross_v(zz, uu):
        at, landed = spot(c, zz, uu, x), spot(c, zz, uu, 1 - x)
        v_cross.append((zz, uu, same(vbuf, at, 1, across, landed)))

    def land_v():
        zz, uu, copy = v_cross.pop(0)
        copy.wait_recv()
        to_sibling(vbuf, spot(c, zz, uu, 0), 2)

    units = (own_u, new_u)

    def pass_on(kind, i, zz, who, landed):
        if kind == K:
            return same(kbuf, spot(c, zz, units[i], 0), 2, who, spot(c, landed, units[i], 0))
        return same(vbuf, spot(c, zz, units[i], x), 1, who, spot(c, landed, units[i], x))

    coming = {(V, 0): (v_up[0], v_down[0])}

    def begin(kind, i):
        coming[kind, i] = (pass_on(kind, i, z, up, ring(-1)), pass_on(kind, i, z, down, ring(1)))

    def advance(kind, i, s):
        from_below, from_above = coming.pop((kind, i))
        lo, hi = ring(-s), ring(s)
        goes_up, goes_down = s < 3 or (s == 3 and i == 0), s < 3 or (s == 3 and i == 1)
        upward = downward = None
        got = []
        if from_below is not None:
            from_below.wait_recv()
            got.append(lo)
            if goes_up:
                upward = pass_on(kind, i, lo, up, ring(-s - 1))
        if from_above is not None:
            from_above.wait_recv()
            got.append(hi)
            if goes_down:
                downward = pass_on(kind, i, hi, down, ring(s + 1))
        coming[kind, i] = (upward, downward)
        for zz in got:
            if kind == K:
                to_sibling(kbuf, spot(c, zz, units[i], 0), 2)
            else:
                cross_v(zz, units[i])

    k_cross.wait_recv()
    begin(K, 0)
    v_swap.wait_recv()
    begin(V, 1)
    cross_v(z, new_u)
    k_swap.wait_recv()
    advance(V, 0, 1)
    later()
    k_diagonal.wait_recv()
    begin(K, 1)
    to_sibling(kbuf, spot(c, z, 0, 0), 4)
    order = ((K, 0, 1), (V, 1, 1), (V, 0, 2), (K, 1, 1), (K, 0, 2), (V, 1, 2), (V, 0, 3), (K, 1, 2), (K, 0, 3), (V, 1, 3),
             (V, 0, 4), (K, 1, 3), (K, 0, 4), (V, 1, 4), (K, 1, 4))
    for kind, i, s in order:
        advance(kind, i, s)
        while len(v_cross) > 4:
            land_v()
    while v_cross:
        land_v()
    for copy in late:
        copy.wait_recv()
    for copy in started:
        copy.wait_send()


COPIES = 80


HALF = 512
CHUNK = 256
EXTRA = 16
UNROLL = 7
ENTRIES = 40


def write_lists(order_ref, mask_ref, lvm, rows, group):
    lane = lax.broadcasted_iota(I32, (8, D), 1)
    slot = lax.broadcasted_iota(I32, (8, D), 0)
    mine = jnp.zeros((8, D), I32)
    for r in range(8):
        mine = jnp.where(slot == r, order_ref[r], mine)
    listed = jnp.logical_and(mask_ref[...] == 1, ((lane >> 2) & 1) == group)
    diagonal = lane == mine
    both = jnp.where(jnp.logical_and(listed, diagonal), 1, 0)
    rank = jnp.where(jnp.logical_and(listed, jnp.logical_not(diagonal)), 1, 0)
    total, has = rank, both
    for k in (1, 2, 4, 8, 16, 32, 64):
        rank = rank + jnp.where(lane >= k, pltpu.roll(rank, k, 1), 0)
        total = total + pltpu.roll(total, k, 1)
        has = has + pltpu.roll(has, k, 1)
    front = jnp.where(diagonal, 0, rank - 1 + has)
    back = jnp.where(diagonal, WIDE * NG - 1, WIDE * NG - rank - has)
    at = jnp.where(listed, jnp.where((slot & 1) == 0, front, back), -1)
    spot = (lane & 1) * 32 + ((lane >> 3) & 7) * 4 + ((lane >> 1) & 1) * 2 + (lane >> 6)
    rows[0] = at
    rows[1] = spot + POOL * jnp.where(diagonal, 1, 0) - 2 * POOL
    rows[2] = jnp.maximum((total + has + WIDE - 1) >> 2, 1)
    place = lax.broadcasted_iota(I32, (ENTRIES, D), 0)
    for p in range(4):
        found = jnp.zeros((ENTRIES, D), I32)
        for j in range(2):
            row = slice(2 * p + j, 2 * p + j + 1)
            found = found + jnp.where(place == rows[0, row], rows[1, row], 0)
        for k in (1, 2, 4, 8, 16, 32, 64):
            found = found + pltpu.roll(found, k, 1)
        first_groups = jnp.broadcast_to(rows[2, 2 * p:2 * p + 1], (ENTRIES, D))
        lvm[p] = jnp.where(place == ENTRIES - 1, first_groups, found + 2 * POOL)


def fused_kernel(order_ref, mask_ref, q_hbm, k_ref, v_ref, out_ref, lvm, table, lsm, kbuf, vbuf, qs, bias, acc, mb, sb, obuf, sbuf, land, lstat,
                 send, recv, local, lsem, qsem, xsend, xrecv, near_sem):
    pb, ka = lax.axis_index("pb"), lax.axis_index("ka")
    x, z = lax.div(pb, RING), lax.rem(pb, RING)
    y, c = lax.div(ka, 2), lax.rem(ka, 2)
    head = head_of(y)

    barrier = pltpu.get_barrier_semaphore()
    partners = [{"ka": lax.rem(ka + d, 8)} for d in range(1, 8)]
    partners += [
        {"pb": (1 - x) * RING + z},
        {"pb": (1 - x) * RING + z, "ka": (y + 1 - 2 * lax.rem(y, 2)) * 2 + c},
        {"pb": x * RING + lax.rem(z + 1, RING)},
        {"pb": x * RING + lax.rem(z + RING - 1, RING)},
    ]
    for who in partners:
        pl.semaphore_signal(barrier, inc=1, device_id=who, device_id_type=MESH)
    pl.semaphore_wait(barrier, len(partners))

    fetch = []
    fetch_lists = pltpu.make_async_copy(lvm, lsm, lsem)
    later = fetch_lists.start

    def meanwhile():
        write_lists(order_ref, mask_ref, lvm, table, lax.div(y, 2))
        for s in range(8):
            for i in range(HALF // D):
                cols = pl.ds(pl.multiple_of(head * LANES + c * HALF + i * D, D), D)
                copy = pltpu.make_async_copy(
                    q_hbm.at[pl.ds(s * D, D), cols], qs.at[s, pl.ds(i * D, D)], qsem.at[s * (HALF // D) + i]
                )
                copy.start()
                fetch.append(copy)
        row = lax.broadcasted_iota(I32, (D, D), 0)
        col = lax.broadcasted_iota(I32, (D, D), 1)
        bias[0] = jnp.zeros((D, D), F32)
        bias[1] = jnp.where(row <= col, 0.0, LOW)
        acc[0] = jnp.zeros(acc.shape[1:], F32)
        mb[0] = jnp.full(mb.shape[1:], LOW, F32)

    gather(k_ref, v_ref, kbuf, vbuf, send, recv, local, meanwhile, later)
    fetch_lists.wait()
    for copy in fetch:
        copy.wait()

    ones = jnp.where(lax.broadcasted_iota(I32, (EXTRA, WIDE * D), 0) == 0, 1.0, 0.0).astype(BF16)

    def entries(p, g):
        return [lsm[p, WIDE * g + k, 0] for k in range(WIDE)]

    def split(p):
        return lsm[p, ENTRIES - 1, 0]

    def scores(p, g, w):
        owner = (g >= split(p)).astype(I32)
        k = jnp.concatenate([kbuf[e & (POOL - 1)] for e in entries(p, g)], axis=0)
        q = qs[2 * p + owner, w:w + CHUNK, :]
        return lax.dot_general(k, q, (((1,), (1,)), ((), ())), preferred_element_type=F32)

    def stage(p, g, diagonal, more=True):
        listed = entries(p, g)
        first = jnp.logical_or(g == 0, g == split(p))
        pads = [e >= 2 * POOL for e in listed]
        v = jnp.concatenate([vbuf[e & (POOL - 1)] for e in listed], axis=0)
        vt = jnp.concatenate([v.T, ones], axis=0)
        now, then = lax.rem(jnp.int32(g), 2), lax.rem(jnp.int32(g) + 1, 2)
        for w in range(0, HALF, CHUNK):
            cut = slice(w, w + CHUNK)
            pieces = [sb[now, k * D:(k + 1) * D, cut] for k in range(WIDE)]
            if more:
                sb[then, :, cut] = scores(p, g + 1, w)
            if diagonal is not None:
                causal = bias[(listed[diagonal] >> 6) & 1]
                pieces[diagonal] = pieces[diagonal] + jnp.concatenate([causal] * (CHUNK // D), axis=1)
            old = jnp.where(first, -3e38, mb[g, 0:1, cut])
            m = old
            for s, pad in zip(pieces, pads):
                m = jnp.maximum(m, jnp.where(pad, LOW, jnp.max(s, axis=0, keepdims=True)))
            alpha = jnp.exp2((old - m) * SCALE)
            weights = [
                jnp.exp2((s - jnp.where(pad, -LOW, m)) * SCALE).astype(BF16) for s, pad in zip(pieces, pads)
            ]
            part = lax.dot_general(
                vt, jnp.concatenate(weights, axis=0), (((1,), (0,)), ((), ())), preferred_element_type=F32
            )
            acc[g + 1, :, cut] = acc[g, :, cut] * alpha + part
            mb[g + 1, 0:1, cut] = m

    odd = lax.rem(y, 2)
    nearby, far, partner = y + 1 - 2 * odd, lax.rem(y + 2, 4), 3 - y
    kinds = ((obuf, land), (sbuf, lstat))

    def part_to(phase, j, kind, target):
        src, dst = kinds[kind]
        n = 2 * phase + j
        return pltpu.make_async_remote_copy(
            src_ref=src.at[n], dst_ref=dst.at[y, c], send_sem=xsend.at[n, kind], recv_sem=xrecv.at[y, c, kind],
            device_id={"ka": target}, device_id_type=MESH,
        )

    def stays(kind):
        src, dst = kinds[kind]
        return pltpu.make_async_copy(src.at[6 + c], dst.at[y, c], near_sem.at[kind])

    def pair_of(phase):
        return jnp.where(phase == 0, far, jnp.where(phase == 1, nearby, jnp.where(phase == 2, partner, y)))

    def run_phase(phase, _):
        p = pair_of(phase)
        for w in range(0, HALF, CHUNK):
            sb[0, :, w:w + CHUNK] = scores(p, 0, w)
        stage(p, 0, 0)

        def step(i, _):
            for t in range(UNROLL):
                stage(p, 1 + i * UNROLL + t, None)
            return 0

        lax.fori_loop(0, (NG - 2) // UNROLL, step, 0)
        stage(p, NG - 1, WIDE - 1, more=False)
        for j in range(2):
            at = split(p) if j == 0 else NG
            obuf[2 * phase + j] = acc[at, 0:D].astype(BF16)
            sbuf[2 * phase + j, 0:1] = mb[at, 0:1]
            sbuf[2 * phase + j, 1:2] = acc[at, D:D + 1]
        for j in range(2):
            mine = jnp.logical_and(phase == 3, c == j)
            for kind in range(2):
                pl.when(jnp.logical_not(mine))(part_to(phase, j, kind, 2 * p + j).start)
                pl.when(mine)(stays(kind).start)
        return 0

    lax.fori_loop(0, 4, run_phase, 0)

    for kv, a, b in ((1 - head, nearby, far), (head, partner, y)):
        for core in range(2):
            for kind in range(2):
                dst = kinds[kind][1]
                for yy in (a, b):
                    come = pltpu.make_async_remote_copy(
                        src_ref=dst.at[yy, core], dst_ref=dst.at[yy, core], send_sem=xsend.at[0, kind],
                        recv_sem=xrecv.at[yy, core, kind], device_id={"ka": lax.rem(ka + 1, 8)}, device_id_type=MESH,
                    )
                    if yy is y:
                        pl.when(core != c)(come.wait_recv)
                        pl.when(core == c)(stays(kind).wait)
                    else:
                        come.wait_recv()
            ma, mb_ = lstat[a, core, 0:1], lstat[b, core, 0:1]
            top = jnp.maximum(ma, mb_)
            fa, fb = jnp.exp2((ma - top) * SCALE), jnp.exp2((mb_ - top) * SCALE)
            whole = fa * lstat[a, core, 1:2] + fb * lstat[b, core, 1:2]
            fa, fb = fa / whole, fb / whole
            for i in range(HALF // D):
                cut = slice(i * D, (i + 1) * D)
                both = land[a, core, :, cut].astype(F32) * fa[:, cut] + land[b, core, :, cut].astype(F32) * fb[:, cut]
                at = pl.multiple_of(kv * LANES + core * HALF + i * D, D)
                out_ref[:, pl.ds(at, D)] = both.T.astype(BF16)
    for phase in range(4):
        for j in range(2):
            for kind in range(2):
                copy = part_to(phase, j, kind, 2 * pair_of(phase) + j)
                if phase < 3:
                    copy.wait_send()
                else:
                    pl.when(c != j)(copy.wait_send)


def fused(q_order, block_mask, queries, keys, values):
    vmem = pl.BlockSpec(memory_space=pltpu.VMEM)
    smem = pl.BlockSpec(memory_space=pltpu.SMEM)
    dma = pltpu.SemaphoreType.DMA
    return pl.pallas_call(
        fused_kernel,
        out_shape=jax.ShapeDtypeStruct((D, 2 * LANES), BF16),
        in_specs=[smem, vmem, pl.BlockSpec(memory_space=pl.ANY), vmem, vmem],
        out_specs=vmem,
        scratch_shapes=[
            pltpu.VMEM((4, ENTRIES, D), I32),
            pltpu.VMEM((3, 8, D), I32),
            pltpu.SMEM((4, ENTRIES, D), I32),
            pltpu.VMEM((POOL, D, D), BF16),
            pltpu.VMEM((POOL, D, D), BF16),
            pltpu.VMEM((8, HALF, D), BF16),
            pltpu.VMEM((2, D, D), F32),
            pltpu.VMEM((NG + 1, D + EXTRA, HALF), F32),
            pltpu.VMEM((NG + 1, 8, HALF), F32),
            pltpu.VMEM((2, WIDE * D, HALF), F32),
            pltpu.VMEM((8, D, HALF), BF16),
            pltpu.VMEM((8, 8, HALF), F32),
            pltpu.VMEM((4, 2, D, HALF), BF16),
            pltpu.VMEM((4, 2, 8, HALF), F32),
            dma((COPIES,)), dma((COPIES,)), dma((2,)), dma(()), dma((8 * HALF // D,)),
            dma((8, 2)), dma((4, 2, 2)), dma((2,)),
        ],
        compiler_params=pltpu.CompilerParams(
            collective_id=0, has_side_effects=True, vmem_limit_bytes=VMEM_LIMIT,
        ),
        name="attend_all",
    )(q_order, block_mask, queries, keys, values)


def on_device(queries, keys, values, q_order, block_mask):
    return fused(q_order, block_mask, queries, keys.reshape(D, 2 * D), values.reshape(D, 2 * D))


def solution(mesh):
    in_specs = (P("pb", "ha"), P("pb", "ka", None, "ha"), P("pb", "ka", None, "ha"), P("pb"), P("pb", None))
    return jax.shard_map(
        on_device, mesh=mesh, in_specs=in_specs, out_specs=P(("pb", "ka"), "ha"), check_vma=False
    )
```

```python
import functools
import math

import jax
import jax.numpy as jnp
from jax import lax
from jax.experimental import pallas as pl
from jax.experimental.pallas import tpu as pltpu
from jax.sharding import PartitionSpec as P

MESH = pl.DeviceIdType.MESH
K, V = 0, 1
BF16, F32, I32 = jnp.bfloat16, jnp.float32, jnp.int32
D = 128
GROUP = 8
LANES = GROUP * D
RING = 8
POOL = 64
NG = 9
WIDE = 4
SCALE = math.log2(math.e) / math.sqrt(D)
LOW = -1e30
VMEM_LIMIT = 60 * 1024 * 1024


def head_of(y):
    return lax.rem(lax.div(y + 1, 2), 2)


def gather(k_ref, v_ref, kbuf, vbuf, send, recv, local, meanwhile, prepare, later):
    pb, ka = lax.axis_index("pb"), lax.axis_index("ka")
    x, z = lax.div(pb, RING), lax.rem(pb, RING)
    y, c = lax.div(ka, 2), lax.rem(ka, 2)
    u = lax.rem(y, 2)
    mate = {"ka": (y + 1 - 2 * u) * 2 + c}
    across = {"pb": (1 - x) * RING + z}
    up = {"pb": x * RING + lax.rem(z + 1, RING)}
    down = {"pb": x * RING + lax.rem(z + RING - 1, RING)}
    sibling = {"ka": y * 2 + 1 - c}
    corner = {"pb": (1 - x) * RING + z, "ka": (y + 1 - 2 * u) * 2 + c}
    head = head_of(y)

    started = []
    number = [0]

    def next_id():
        number[0] += 1
        return number[0] - 1

    def move(src, dst, landed, who):
        n = next_id()
        copy = pltpu.make_async_remote_copy(
            src_ref=src, dst_ref=dst, send_sem=send.at[n], recv_sem=recv.at[n],
            device_id=who, device_id_type=MESH,
        )
        copy.start()
        started.append(copy)
        return pltpu.make_async_remote_copy(
            src_ref=src, dst_ref=landed, send_sem=send.at[n], recv_sem=recv.at[n],
            device_id=who, device_id_type=MESH,
        )

    def ring(s):
        return lax.rem(z + s + RING, RING)

    def spot(core, zz, uu, xx):
        return ((core * RING + zz) * 2 + uu) * 2 + xx

    late = []

    def blocks(buf, at, count):
        return buf.at[pl.ds(at, count)]

    def same(buf, at, count, who, landed):
        return move(blocks(buf, at, count), blocks(buf, at, count), blocks(buf, landed, count), who)

    def to_sibling(buf, at, count):
        late.append(same(buf, at, count, sibling, at + (1 - 2 * c) * (POOL // 2)))

    own_u, new_u = u, 1 - u
    own, new = spot(c, z, own_u, x), spot(c, z, new_u, x)
    ours = pl.ds(pl.multiple_of(head * D, D), D)
    theirs = pl.ds(pl.multiple_of((1 - head) * D, D), D)
    k_swap = move(k_ref.at[:, theirs], kbuf.at[own], kbuf.at[new], mate)
    v_swap = move(v_ref.at[:, theirs], vbuf.at[own], vbuf.at[new], mate)
    k_cross = move(k_ref.at[:, ours], kbuf.at[own], kbuf.at[spot(c, z, own_u, 1 - x)], across)
    k_diagonal = move(k_ref.at[:, theirs], kbuf.at[own], kbuf.at[spot(c, z, new_u, 1 - x)], corner)
    v_up = [move(v_ref.at[:, ours], vbuf.at[own], vbuf.at[spot(c, ring(-1), own_u, x)], up)]
    v_down = [move(v_ref.at[:, ours], vbuf.at[own], vbuf.at[spot(c, ring(1), own_u, x)], down)]
    v_cross = [(z, own_u, move(v_ref.at[:, ours], vbuf.at[own], vbuf.at[spot(c, z, own_u, 1 - x)], across))]
    mine = [
        pltpu.make_async_copy(r.at[:, ours], b.at[own], local.at[i])
        for i, (r, b) in enumerate(((k_ref, kbuf), (v_ref, vbuf)))
    ]
    for copy in mine:
        copy.start()
    meanwhile()
    for copy in mine:
        copy.wait()

    def cross_v(zz, uu):
        at, landed = spot(c, zz, uu, x), spot(c, zz, uu, 1 - x)
        v_cross.append((zz, uu, same(vbuf, at, 1, across, landed)))

    def land_v():
        zz, uu, copy = v_cross.pop(0)
        copy.wait_recv()
        to_sibling(vbuf, spot(c, zz, uu, 0), 2)

    units = (own_u, new_u)

    def pass_on(kind, i, zz, who, landed):
        if kind == K:
            return same(kbuf, spot(c, zz, units[i], 0), 2, who, spot(c, landed, units[i], 0))
        return same(vbuf, spot(c, zz, units[i], x), 1, who, spot(c, landed, units[i], x))

    coming = {(V, 0): (v_up[0], v_down[0])}

    def begin(kind, i):
        coming[kind, i] = (pass_on(kind, i, z, up, ring(-1)), pass_on(kind, i, z, down, ring(1)))

    def advance(kind, i, s):
        from_below, from_above = coming.pop((kind, i))
        lo, hi = ring(-s), ring(s)
        goes_up, goes_down = s < 3 or (s == 3 and i == 0), s < 3 or (s == 3 and i == 1)
        upward = downward = None
        got = []
        if from_below is not None:
            from_below.wait_recv()
            got.append(lo)
            if goes_up:
                upward = pass_on(kind, i, lo, up, ring(-s - 1))
        if from_above is not None:
            from_above.wait_recv()
            got.append(hi)
            if goes_down:
                downward = pass_on(kind, i, hi, down, ring(s + 1))
        coming[kind, i] = (upward, downward)
        for zz in got:
            if kind == V:
                cross_v(zz, units[i])
            elif i == 1 and s < 4:
                to_sibling(kbuf, spot(c, zz, 0, 0), 4)
            elif i == 1:
                to_sibling(kbuf, spot(c, zz, new_u, 0), 2)
            elif s == 4:
                to_sibling(kbuf, spot(c, zz, own_u, 0), 2)

    k_cross.wait_recv()
    begin(K, 0)
    v_swap.wait_recv()
    begin(V, 1)
    cross_v(z, new_u)
    k_swap.wait_recv()
    advance(V, 0, 1)
    k_diagonal.wait_recv()
    begin(K, 1)
    to_sibling(kbuf, spot(c, z, 0, 0), 4)
    prepare()
    order = ((K, 0, 1), (V, 1, 1), (V, 0, 2), (K, 1, 1), (K, 0, 2), (V, 1, 2), (V, 0, 3), (K, 1, 2), (K, 0, 3), (V, 1, 3),
             (V, 0, 4), (K, 1, 3), (K, 0, 4), (V, 1, 4), (K, 1, 4))
    for kind, i, s in order:
        advance(kind, i, s)
        if (kind, i, s) == (V, 0, 3):
            later()
        while len(v_cross) > 4:
            land_v()
    while v_cross:
        land_v()
    for copy in late:
        copy.wait_recv()
    return started


COPIES = 80


HALF = 512
CHUNK = 512
EXTRA = 16
UNROLL = 7
ENTRIES = 40


def write_lists(order_ref, mask_ref, lvm, rows, group):
    lane = lax.broadcasted_iota(I32, (8, D), 1)
    slot = lax.broadcasted_iota(I32, (8, D), 0)
    mine = jnp.zeros((8, D), I32)
    for r in range(8):
        mine = jnp.where(slot == r, order_ref[r], mine)
    listed = jnp.logical_and(mask_ref[...] == 1, ((lane >> 2) & 1) == group)
    diagonal = lane == mine
    both = jnp.where(jnp.logical_and(listed, diagonal), 1, 0)
    rank = jnp.where(jnp.logical_and(listed, jnp.logical_not(diagonal)), 1, 0)
    total, has = rank, both
    for k in (1, 2, 4, 8, 16, 32, 64):
        rank = rank + jnp.where(lane >= k, pltpu.roll(rank, k, 1), 0)
        total = total + pltpu.roll(total, k, 1)
        has = has + pltpu.roll(has, k, 1)
    front = jnp.where(diagonal, 0, rank - 1 + has)
    back = jnp.where(diagonal, WIDE * NG - 1, WIDE * NG - rank - has)
    at = jnp.where(listed, jnp.where((slot & 1) == 0, front, back), -1)
    spot = (lane & 1) * 32 + ((lane >> 3) & 7) * 4 + ((lane >> 1) & 1) * 2 + (lane >> 6)
    rows[0] = at
    rows[1] = spot + POOL * jnp.where(diagonal, 1, 0) - 2 * POOL
    rows[2] = jnp.maximum((total + has + WIDE - 1) >> 2, 1)
    place = lax.broadcasted_iota(I32, (ENTRIES, D), 0)
    for p in range(4):
        found = jnp.zeros((ENTRIES, D), I32)
        for j in range(2):
            row = slice(2 * p + j, 2 * p + j + 1)
            found = found + jnp.where(place == rows[0, row], rows[1, row], 0)
        for k in (1, 2, 4, 8, 16, 32, 64):
            found = found + pltpu.roll(found, k, 1)
        first_groups = jnp.broadcast_to(rows[2, 2 * p:2 * p + 1], (ENTRIES, D))
        lvm[p] = jnp.where(place == ENTRIES - 1, first_groups, found + 2 * POOL)


def fused_kernel(order_ref, mask_ref, q_hbm, k_ref, v_ref, out_ref, lvm, table, lsm, kbuf, vbuf, qs, bias, acc, mb, sb, obuf, sbuf, land, lstat,
                 send, recv, local, lsem, qsem, xsend, xrecv, near_sem):
    pb, ka = lax.axis_index("pb"), lax.axis_index("ka")
    x, z = lax.div(pb, RING), lax.rem(pb, RING)
    y, c = lax.div(ka, 2), lax.rem(ka, 2)
    head = head_of(y)

    barrier = pltpu.get_barrier_semaphore()
    partners = [{"ka": lax.rem(ka + d, 8)} for d in range(1, 8)]
    partners += [
        {"pb": (1 - x) * RING + z},
        {"pb": (1 - x) * RING + z, "ka": (y + 1 - 2 * lax.rem(y, 2)) * 2 + c},
        {"pb": x * RING + lax.rem(z + 1, RING)},
        {"pb": x * RING + lax.rem(z + RING - 1, RING)},
    ]
    for who in partners:
        pl.semaphore_signal(barrier, inc=1, device_id=who, device_id_type=MESH)
    pl.semaphore_wait(barrier, len(partners))

    fetch = []
    fetch_lists = pltpu.make_async_copy(lvm, lsm, lsem)
    later = fetch_lists.start

    def prepare():
        write_lists(order_ref, mask_ref, lvm, table, lax.div(y, 2))

    def meanwhile():
        for s in range(8):
            for i in range(HALF // D):
                cols = pl.ds(pl.multiple_of(head * LANES + c * HALF + i * D, D), D)
                copy = pltpu.make_async_copy(
                    q_hbm.at[pl.ds(s * D, D), cols], qs.at[s, pl.ds(i * D, D)], qsem.at[s * (HALF // D) + i]
                )
                copy.start()
                fetch.append(copy)
        row = lax.broadcasted_iota(I32, (D, D), 0)
        col = lax.broadcasted_iota(I32, (D, D), 1)
        bias[0] = jnp.zeros((D, D), F32)
        bias[1] = jnp.where(row <= col, 0.0, LOW)
        acc[0] = jnp.zeros(acc.shape[1:], F32)
        mb[0] = jnp.full(mb.shape[1:], LOW, F32)

    gathered = gather(k_ref, v_ref, kbuf, vbuf, send, recv, local, meanwhile, prepare, later)
    fetch_lists.wait()
    for copy in fetch:
        copy.wait()

    ones = jnp.where(lax.broadcasted_iota(I32, (EXTRA, WIDE * D), 0) == 0, 1.0, 0.0).astype(BF16)

    def entries(p, g):
        return [lsm[p, WIDE * g + k, 0] for k in range(WIDE)]

    def split(p):
        return lsm[p, ENTRIES - 1, 0]

    def scores(p, g, w):
        owner = (g >= split(p)).astype(I32)
        k = jnp.concatenate([kbuf[e & (POOL - 1)] for e in entries(p, g)], axis=0)
        q = qs[2 * p + owner, w:w + CHUNK, :]
        return lax.dot_general(k, q, (((1,), (1,)), ((), ())), preferred_element_type=F32)

    def stage(p, g, diagonal, more=True):
        listed = entries(p, g)
        first = jnp.logical_or(g == 0, g == split(p))
        pads = [e >= 2 * POOL for e in listed]
        v = jnp.concatenate([vbuf[e & (POOL - 1)] for e in listed], axis=0)
        vt = jnp.concatenate([v.T, ones], axis=0)
        now, then = lax.rem(jnp.int32(g), 2), lax.rem(jnp.int32(g) + 1, 2)
        for w in range(0, HALF, CHUNK):
            cut = slice(w, w + CHUNK)
            pieces = [sb[now, k * D:(k + 1) * D, cut] for k in range(WIDE)]
            if more:
                sb[then, :, cut] = scores(p, g + 1, w)
            if diagonal is not None:
                causal = bias[(listed[diagonal] >> 6) & 1]
                pieces[diagonal] = pieces[diagonal] + jnp.concatenate([causal] * (CHUNK // D), axis=1)
            old = jnp.where(first, -3e38, mb[g, 0:1, cut])
            m = old
            for s, pad in zip(pieces, pads):
                m = jnp.maximum(m, jnp.where(pad, LOW, jnp.max(s, axis=0, keepdims=True)))
            alpha = jnp.exp2((old - m) * SCALE)
            weights = [
                jnp.exp2((s - jnp.where(pad, -LOW, m)) * SCALE).astype(BF16) for s, pad in zip(pieces, pads)
            ]
            part = lax.dot_general(
                vt, jnp.concatenate(weights, axis=0), (((1,), (0,)), ((), ())), preferred_element_type=F32
            )
            acc[g + 1, :, cut] = acc[g, :, cut] * alpha + part
            mb[g + 1, 0:1, cut] = m

    odd = lax.rem(y, 2)
    nearby, far, partner = y + 1 - 2 * odd, lax.rem(y + 2, 4), 3 - y
    kinds = ((obuf, land), (sbuf, lstat))

    def part_to(phase, j, kind, target):
        src, dst = kinds[kind]
        n = 2 * phase + j
        return pltpu.make_async_remote_copy(
            src_ref=src.at[n], dst_ref=dst.at[y, c], send_sem=xsend.at[n, kind], recv_sem=xrecv.at[y, c, kind],
            device_id={"ka": target}, device_id_type=MESH,
        )

    def stays(kind):
        src, dst = kinds[kind]
        return pltpu.make_async_copy(src.at[6 + c], dst.at[y, c], near_sem.at[kind])

    second, third = jnp.where(c == 0, nearby, partner), jnp.where(c == 0, partner, nearby)

    def pair_of(phase):
        return jnp.where(phase == 0, far, jnp.where(phase == 1, second, jnp.where(phase == 2, third, y)))

    def run_phase(phase, _):
        p = pair_of(phase)
        for w in range(0, HALF, CHUNK):
            sb[0, :, w:w + CHUNK] = scores(p, 0, w)
        stage(p, 0, 0)

        def step(i, _):
            for t in range(UNROLL):
                stage(p, 1 + i * UNROLL + t, None)
            return 0

        lax.fori_loop(0, (NG - 2) // UNROLL, step, 0)
        stage(p, NG - 1, WIDE - 1, more=False)
        for j in range(2):
            at = split(p) if j == 0 else NG
            obuf[2 * phase + j] = acc[at, 0:D].astype(BF16)
            sbuf[2 * phase + j, 0:1] = mb[at, 0:1]
            sbuf[2 * phase + j, 1:2] = acc[at, D:D + 1]
        for j in range(2):
            mine = jnp.logical_and(phase == 3, c == j)
            for kind in range(2):
                pl.when(jnp.logical_not(mine))(part_to(phase, j, kind, 2 * p + j).start)
                pl.when(mine)(stays(kind).start)
        return 0

    lax.fori_loop(0, 4, run_phase, 0)

    for kv, a, b in ((1 - head, nearby, far), (head, partner, y)):
        for core in range(2):
            for kind in range(2):
                dst = kinds[kind][1]
                for yy in (a, b):
                    come = pltpu.make_async_remote_copy(
                        src_ref=dst.at[yy, core], dst_ref=dst.at[yy, core], send_sem=xsend.at[0, kind],
                        recv_sem=xrecv.at[yy, core, kind], device_id={"ka": lax.rem(ka + 1, 8)}, device_id_type=MESH,
                    )
                    if yy is y:
                        pl.when(core != c)(come.wait_recv)
                        pl.when(core == c)(stays(kind).wait)
                    else:
                        come.wait_recv()
            ma, mb_ = lstat[a, core, 0:1], lstat[b, core, 0:1]
            top = jnp.maximum(ma, mb_)
            fa, fb = jnp.exp2((ma - top) * SCALE), jnp.exp2((mb_ - top) * SCALE)
            whole = fa * lstat[a, core, 1:2] + fb * lstat[b, core, 1:2]
            fa, fb = fa / whole, fb / whole
            for i in range(HALF // D):
                cut = slice(i * D, (i + 1) * D)
                both = land[a, core, :, cut].astype(F32) * fa[:, cut] + land[b, core, :, cut].astype(F32) * fb[:, cut]
                at = pl.multiple_of(kv * LANES + core * HALF + i * D, D)
                out_ref[:, pl.ds(at, D)] = both.T.astype(BF16)
    for copy in gathered:
        copy.wait_send()
    for phase in range(4):
        for j in range(2):
            for kind in range(2):
                copy = part_to(phase, j, kind, 2 * pair_of(phase) + j)
                if phase < 3:
                    copy.wait_send()
                else:
                    pl.when(c != j)(copy.wait_send)


def fused(q_order, block_mask, queries, keys, values):
    vmem = pl.BlockSpec(memory_space=pltpu.VMEM)
    smem = pl.BlockSpec(memory_space=pltpu.SMEM)
    dma = pltpu.SemaphoreType.DMA
    return pl.pallas_call(
        fused_kernel,
        out_shape=jax.ShapeDtypeStruct((D, 2 * LANES), BF16),
        in_specs=[smem, vmem, pl.BlockSpec(memory_space=pl.ANY), vmem, vmem],
        out_specs=vmem,
        scratch_shapes=[
            pltpu.VMEM((4, ENTRIES, D), I32),
            pltpu.VMEM((3, 8, D), I32),
            pltpu.SMEM((4, ENTRIES, D), I32),
            pltpu.VMEM((POOL, D, D), BF16),
            pltpu.VMEM((POOL, D, D), BF16),
            pltpu.VMEM((8, HALF, D), BF16),
            pltpu.VMEM((2, D, D), F32),
            pltpu.VMEM((NG + 1, D + EXTRA, HALF), F32),
            pltpu.VMEM((NG + 1, 8, HALF), F32),
            pltpu.VMEM((2, WIDE * D, HALF), F32),
            pltpu.VMEM((8, D, HALF), BF16),
            pltpu.VMEM((8, 8, HALF), F32),
            pltpu.VMEM((4, 2, D, HALF), BF16),
            pltpu.VMEM((4, 2, 8, HALF), F32),
            dma((COPIES,)), dma((COPIES,)), dma((2,)), dma(()), dma((8 * HALF // D,)),
            dma((8, 2)), dma((4, 2, 2)), dma((2,)),
        ],
        compiler_params=pltpu.CompilerParams(
            collective_id=0, has_side_effects=True, vmem_limit_bytes=VMEM_LIMIT,
        ),
        name="attend_all",
    )(q_order, block_mask, queries, keys, values)


def on_device(queries, keys, values, q_order, block_mask):
    return fused(q_order, block_mask, queries, keys.reshape(D, 2 * D), values.reshape(D, 2 * D))


def solution(mesh):
    in_specs = (P("pb", "ha"), P("pb", "ka", None, "ha"), P("pb", "ka", None, "ha"), P("pb"), P("pb", None))
    return jax.shard_map(
        on_device, mesh=mesh, in_specs=in_specs, out_specs=P(("pb", "ka"), "ha"), check_vma=False
    )
```

```python
import functools
import math

import jax
import jax.numpy as jnp
from jax import lax
from jax.experimental import pallas as pl
from jax.experimental.pallas import tpu as pltpu
from jax.sharding import PartitionSpec as P

MESH = pl.DeviceIdType.MESH
K, V = 0, 1
BF16, F32, I32 = jnp.bfloat16, jnp.float32, jnp.int32
D = 128
GROUP = 8
LANES = GROUP * D
RING = 8
POOL = 64
NG = 9
WIDE = 4
SCALE = math.log2(math.e) / math.sqrt(D)
LOW = -1e30
VMEM_LIMIT = 60 * 1024 * 1024


def head_of(y):
    return lax.rem(lax.div(y + 1, 2), 2)


def gather(k_ref, v_ref, kbuf, vbuf, send, recv, local, meanwhile, prepare, later):
    pb, ka = lax.axis_index("pb"), lax.axis_index("ka")
    x, z = lax.div(pb, RING), lax.rem(pb, RING)
    y, c = lax.div(ka, 2), lax.rem(ka, 2)
    u = lax.rem(y, 2)
    mate = {"ka": (y + 1 - 2 * u) * 2 + c}
    across = {"pb": (1 - x) * RING + z}
    up = {"pb": x * RING + lax.rem(z + 1, RING)}
    down = {"pb": x * RING + lax.rem(z + RING - 1, RING)}
    sibling = {"ka": y * 2 + 1 - c}
    corner = {"pb": (1 - x) * RING + z, "ka": (y + 1 - 2 * u) * 2 + c}
    head = head_of(y)

    started = []
    number = [0]

    def next_id():
        number[0] += 1
        return number[0] - 1

    def move(src, dst, landed, who):
        n = next_id()
        copy = pltpu.make_async_remote_copy(
            src_ref=src, dst_ref=dst, send_sem=send.at[n], recv_sem=recv.at[n],
            device_id=who, device_id_type=MESH,
        )
        copy.start()
        started.append(copy)
        return pltpu.make_async_remote_copy(
            src_ref=src, dst_ref=landed, send_sem=send.at[n], recv_sem=recv.at[n],
            device_id=who, device_id_type=MESH,
        )

    def ring(s):
        return lax.rem(z + s + RING, RING)

    def spot(core, zz, uu, xx):
        return ((core * RING + zz) * 2 + uu) * 2 + xx

    late = []

    def blocks(buf, at, count):
        return buf.at[pl.ds(at, count)]

    def same(buf, at, count, who, landed):
        return move(blocks(buf, at, count), blocks(buf, at, count), blocks(buf, landed, count), who)

    def to_sibling(buf, at, count):
        late.append(same(buf, at, count, sibling, at + (1 - 2 * c) * (POOL // 2)))

    own_u, new_u = u, 1 - u
    own, new = spot(c, z, own_u, x), spot(c, z, new_u, x)
    ours = pl.ds(pl.multiple_of(head * D, D), D)
    theirs = pl.ds(pl.multiple_of((1 - head) * D, D), D)
    k_swap = move(k_ref.at[:, theirs], kbuf.at[own], kbuf.at[new], mate)
    v_swap = move(v_ref.at[:, theirs], vbuf.at[own], vbuf.at[new], mate)
    k_cross = move(k_ref.at[:, ours], kbuf.at[own], kbuf.at[spot(c, z, own_u, 1 - x)], across)
    k_diagonal = move(k_ref.at[:, theirs], kbuf.at[own], kbuf.at[spot(c, z, new_u, 1 - x)], corner)
    v_up = [move(v_ref.at[:, ours], vbuf.at[own], vbuf.at[spot(c, ring(-1), own_u, x)], up)]
    v_down = [move(v_ref.at[:, ours], vbuf.at[own], vbuf.at[spot(c, ring(1), own_u, x)], down)]
    v_cross = [(z, own_u, move(v_ref.at[:, ours], vbuf.at[own], vbuf.at[spot(c, z, own_u, 1 - x)], across))]
    mine = [
        pltpu.make_async_copy(r.at[:, ours], b.at[own], local.at[i])
        for i, (r, b) in enumerate(((k_ref, kbuf), (v_ref, vbuf)))
    ]
    for copy in mine:
        copy.start()
    meanwhile()
    for copy in mine:
        copy.wait()

    def cross_v(zz, uu):
        at, landed = spot(c, zz, uu, x), spot(c, zz, uu, 1 - x)
        v_cross.append((zz, uu, same(vbuf, at, 1, across, landed)))

    def land_v():
        zz, uu, copy = v_cross.pop(0)
        copy.wait_recv()
        to_sibling(vbuf, spot(c, zz, uu, 0), 2)

    units = (own_u, new_u)

    def pass_on(kind, i, zz, who, landed):
        if kind == K:
            return same(kbuf, spot(c, zz, units[i], 0), 2, who, spot(c, landed, units[i], 0))
        return same(vbuf, spot(c, zz, units[i], x), 1, who, spot(c, landed, units[i], x))

    coming = {(V, 0): (v_up[0], v_down[0])}

    def begin(kind, i):
        coming[kind, i] = (pass_on(kind, i, z, up, ring(-1)), pass_on(kind, i, z, down, ring(1)))

    def advance(kind, i, s):
        from_below, from_above = coming.pop((kind, i))
        lo, hi = ring(-s), ring(s)
        goes_up, goes_down = s < 3 or (s == 3 and i == 0), s < 3 or (s == 3 and i == 1)
        upward = downward = None
        got = []
        if from_below is not None:
            from_below.wait_recv()
            got.append(lo)
            if goes_up:
                upward = pass_on(kind, i, lo, up, ring(-s - 1))
        if from_above is not None:
            from_above.wait_recv()
            got.append(hi)
            if goes_down:
                downward = pass_on(kind, i, hi, down, ring(s + 1))
        coming[kind, i] = (upward, downward)
        for zz in got:
            if kind == V:
                cross_v(zz, units[i])
            elif i == 1 and s < 4:
                to_sibling(kbuf, spot(c, zz, 0, 0), 4)
            elif i == 1:
                to_sibling(kbuf, spot(c, zz, new_u, 0), 2)
            elif s == 4:
                to_sibling(kbuf, spot(c, zz, own_u, 0), 2)

    k_cross.wait_recv()
    begin(K, 0)
    v_swap.wait_recv()
    begin(V, 1)
    cross_v(z, new_u)
    k_swap.wait_recv()
    advance(V, 0, 1)
    k_diagonal.wait_recv()
    begin(K, 1)
    to_sibling(kbuf, spot(c, z, 0, 0), 4)
    prepare()
    order = ((K, 0, 1), (V, 1, 1), (V, 0, 2), (K, 1, 1), (K, 0, 2), (V, 1, 2), (V, 0, 3), (K, 1, 2), (K, 0, 3), (V, 1, 3),
             (V, 0, 4), (K, 1, 3), (K, 0, 4), (V, 1, 4), (K, 1, 4))
    for kind, i, s in order:
        advance(kind, i, s)
        if (kind, i, s) == (V, 0, 3):
            later()
        while len(v_cross) > 4:
            land_v()
    while v_cross:
        land_v()
    for copy in late:
        copy.wait_recv()
    return started


COPIES = 80


HALF = 512
CHUNK = 512
EXTRA = 16
ENTRIES = 40


def write_lists(order_ref, mask_ref, lvm, rows, group):
    lane = lax.broadcasted_iota(I32, (8, D), 1)
    slot = lax.broadcasted_iota(I32, (8, D), 0)
    mine = jnp.zeros((8, D), I32)
    for r in range(8):
        mine = jnp.where(slot == r, order_ref[r], mine)
    listed = jnp.logical_and(mask_ref[...] == 1, ((lane >> 2) & 1) == group)
    diagonal = lane == mine
    both = jnp.where(jnp.logical_and(listed, diagonal), 1, 0)
    rank = jnp.where(jnp.logical_and(listed, jnp.logical_not(diagonal)), 1, 0)
    total, has = rank, both
    for k in (1, 2, 4, 8, 16, 32, 64):
        rank = rank + jnp.where(lane >= k, pltpu.roll(rank, k, 1), 0)
        total = total + pltpu.roll(total, k, 1)
        has = has + pltpu.roll(has, k, 1)
    front = jnp.where(diagonal, 0, rank - 1 + has)
    back = jnp.where(diagonal, WIDE * NG - 1, WIDE * NG - rank - has)
    at = jnp.where(listed, jnp.where((slot & 1) == 0, front, back), -1)
    spot = (lane & 1) * 32 + ((lane >> 3) & 7) * 4 + ((lane >> 1) & 1) * 2 + (lane >> 6)
    rows[0] = at
    rows[1] = spot + POOL * jnp.where(diagonal, 1, 0) - 2 * POOL
    rows[2] = jnp.maximum((total + has + WIDE - 1) >> 2, 1)
    place = lax.broadcasted_iota(I32, (ENTRIES, D), 0)
    for p in range(4):
        found = jnp.zeros((ENTRIES, D), I32)
        for j in range(2):
            row = slice(2 * p + j, 2 * p + j + 1)
            found = found + jnp.where(place == rows[0, row], rows[1, row], 0)
        for k in (1, 2, 4, 8, 16, 32, 64):
            found = found + pltpu.roll(found, k, 1)
        first_groups = jnp.broadcast_to(rows[2, 2 * p:2 * p + 1], (ENTRIES, D))
        lvm[p] = jnp.where(place == ENTRIES - 1, first_groups, found + 2 * POOL)


def fused_kernel(order_ref, mask_ref, q_hbm, k_ref, v_ref, out_ref, lvm, table, lsm, kbuf, vbuf, qs, bias, acc, mb, sb, obuf, sbuf, land, lstat,
                 send, recv, local, lsem, qsem, xsend, xrecv, near_sem):
    pb, ka = lax.axis_index("pb"), lax.axis_index("ka")
    x, z = lax.div(pb, RING), lax.rem(pb, RING)
    y, c = lax.div(ka, 2), lax.rem(ka, 2)
    head = head_of(y)

    barrier = pltpu.get_barrier_semaphore()
    partners = [{"ka": lax.rem(ka + d, 8)} for d in range(1, 8)]
    partners += [
        {"pb": (1 - x) * RING + z},
        {"pb": (1 - x) * RING + z, "ka": (y + 1 - 2 * lax.rem(y, 2)) * 2 + c},
        {"pb": x * RING + lax.rem(z + 1, RING)},
        {"pb": x * RING + lax.rem(z + RING - 1, RING)},
    ]
    for who in partners:
        pl.semaphore_signal(barrier, inc=1, device_id=who, device_id_type=MESH)
    pl.semaphore_wait(barrier, len(partners))

    fetch = []
    fetch_lists = pltpu.make_async_copy(lvm, lsm, lsem)
    later = fetch_lists.start

    def prepare():
        write_lists(order_ref, mask_ref, lvm, table, lax.div(y, 2))

    def meanwhile():
        for s in range(8):
            for i in range(HALF // D):
                cols = pl.ds(pl.multiple_of(head * LANES + c * HALF + i * D, D), D)
                copy = pltpu.make_async_copy(
                    q_hbm.at[pl.ds(s * D, D), cols], qs.at[s, pl.ds(i * D, D)], qsem.at[s * (HALF // D) + i]
                )
                copy.start()
                fetch.append(copy)
        row = lax.broadcasted_iota(I32, (D, D), 0)
        col = lax.broadcasted_iota(I32, (D, D), 1)
        bias[0] = jnp.zeros((D, D), F32)
        bias[1] = jnp.where(row <= col, 0.0, LOW)
        acc[0] = jnp.zeros(acc.shape[1:], F32)
        mb[0] = jnp.full(mb.shape[1:], LOW, F32)

    gathered = gather(k_ref, v_ref, kbuf, vbuf, send, recv, local, meanwhile, prepare, later)
    fetch_lists.wait()
    for copy in fetch:
        copy.wait()

    ones = jnp.where(lax.broadcasted_iota(I32, (EXTRA, WIDE * D), 0) == 0, 1.0, 0.0).astype(BF16)

    def entries(p, g):
        return [lsm[p, WIDE * g + k, 0] for k in range(WIDE)]

    def split(p):
        return lsm[p, ENTRIES - 1, 0]

    def scores(p, g, w):
        owner = (g >= split(p)).astype(I32)
        k = jnp.concatenate([kbuf[e & (POOL - 1)] for e in entries(p, g)], axis=0)
        q = qs[2 * p + owner, w:w + CHUNK, :]
        return lax.dot_general(k, q, (((1,), (1,)), ((), ())), preferred_element_type=F32)

    def stage(p, g, diagonal, more=True):
        listed = entries(p, g)
        first = jnp.logical_or(g == 0, g == split(p))
        pads = [e >= 2 * POOL for e in listed]
        v = jnp.concatenate([vbuf[e & (POOL - 1)] for e in listed], axis=0)
        vt = jnp.concatenate([v.T, ones], axis=0)
        now, then = g % 2, (g + 1) % 2
        for w in range(0, HALF, CHUNK):
            cut = slice(w, w + CHUNK)
            pieces = [sb[now, k * D:(k + 1) * D, cut] for k in range(WIDE)]
            if more:
                sb[then, :, cut] = scores(p, g + 1, w)
            if diagonal is not None:
                causal = bias[(listed[diagonal] >> 6) & 1]
                pieces[diagonal] = pieces[diagonal] + jnp.concatenate([causal] * (CHUNK // D), axis=1)
            old = jnp.where(first, -3e38, mb[g, 0:1, cut])
            m = old
            for s, pad in zip(pieces, pads):
                m = jnp.maximum(m, jnp.where(pad, LOW, jnp.max(s, axis=0, keepdims=True)))
            alpha = jnp.exp2((old - m) * SCALE)
            weights = [
                jnp.exp2((s - jnp.where(pad, -LOW, m)) * SCALE).astype(BF16) for s, pad in zip(pieces, pads)
            ]
            part = lax.dot_general(
                vt, jnp.concatenate(weights, axis=0), (((1,), (0,)), ((), ())), preferred_element_type=F32
            )
            acc[g + 1, :, cut] = acc[g, :, cut] * alpha + part
            mb[g + 1, 0:1, cut] = m

    odd = lax.rem(y, 2)
    nearby, far, partner = y + 1 - 2 * odd, lax.rem(y + 2, 4), 3 - y
    kinds = ((obuf, land), (sbuf, lstat))

    def part_to(phase, j, kind, target):
        src, dst = kinds[kind]
        n = 2 * phase + j
        return pltpu.make_async_remote_copy(
            src_ref=src.at[n], dst_ref=dst.at[y, c], send_sem=xsend.at[n, kind], recv_sem=xrecv.at[y, c, kind],
            device_id={"ka": target}, device_id_type=MESH,
        )

    def stays(kind):
        src, dst = kinds[kind]
        return pltpu.make_async_copy(src.at[6 + c], dst.at[y, c], near_sem.at[kind])

    second, third = jnp.where(c == 0, nearby, partner), jnp.where(c == 0, partner, nearby)

    def pair_of(phase):
        return jnp.where(phase == 0, far, jnp.where(phase == 1, second, jnp.where(phase == 2, third, y)))

    def run_phase(phase, _):
        p = pair_of(phase)
        for w in range(0, HALF, CHUNK):
            sb[0, :, w:w + CHUNK] = scores(p, 0, w)
        stage(p, 0, 0)

        for g in range(1, NG - 1):
            stage(p, g, None)
        stage(p, NG - 1, WIDE - 1, more=False)
        for j in range(2):
            at = split(p) if j == 0 else NG
            obuf[2 * phase + j] = acc[at, 0:D].astype(BF16)
            sbuf[2 * phase + j, 0:1] = mb[at, 0:1]
            sbuf[2 * phase + j, 1:2] = acc[at, D:D + 1]
        for j in range(2):
            mine = jnp.logical_and(phase == 3, c == j)
            for kind in range(2):
                pl.when(jnp.logical_not(mine))(part_to(phase, j, kind, 2 * p + j).start)
                pl.when(mine)(stays(kind).start)
        return 0

    lax.fori_loop(0, 4, run_phase, 0)

    for kv, a, b in ((1 - head, nearby, far), (head, partner, y)):
        for core in range(2):
            for kind in range(2):
                dst = kinds[kind][1]
                for yy in (a, b):
                    come = pltpu.make_async_remote_copy(
                        src_ref=dst.at[yy, core], dst_ref=dst.at[yy, core], send_sem=xsend.at[0, kind],
                        recv_sem=xrecv.at[yy, core, kind], device_id={"ka": lax.rem(ka + 1, 8)}, device_id_type=MESH,
                    )
                    if yy is y:
                        pl.when(core != c)(come.wait_recv)
                        pl.when(core == c)(stays(kind).wait)
                    else:
                        come.wait_recv()
            ma, mb_ = lstat[a, core, 0:1], lstat[b, core, 0:1]
            top = jnp.maximum(ma, mb_)
            fa, fb = jnp.exp2((ma - top) * SCALE), jnp.exp2((mb_ - top) * SCALE)
            whole = fa * lstat[a, core, 1:2] + fb * lstat[b, core, 1:2]
            fa, fb = fa / whole, fb / whole
            for i in range(HALF // D):
                cut = slice(i * D, (i + 1) * D)
                both = land[a, core, :, cut].astype(F32) * fa[:, cut] + land[b, core, :, cut].astype(F32) * fb[:, cut]
                at = pl.multiple_of(kv * LANES + core * HALF + i * D, D)
                out_ref[:, pl.ds(at, D)] = both.astype(BF16).T
    for copy in gathered:
        copy.wait_send()
    for phase in range(4):
        for j in range(2):
            for kind in range(2):
                copy = part_to(phase, j, kind, 2 * pair_of(phase) + j)
                if phase < 3:
                    copy.wait_send()
                else:
                    pl.when(c != j)(copy.wait_send)


def fused(q_order, block_mask, queries, keys, values):
    vmem = pl.BlockSpec(memory_space=pltpu.VMEM)
    smem = pl.BlockSpec(memory_space=pltpu.SMEM)
    dma = pltpu.SemaphoreType.DMA
    return pl.pallas_call(
        fused_kernel,
        out_shape=jax.ShapeDtypeStruct((D, 2 * LANES), BF16),
        in_specs=[smem, vmem, pl.BlockSpec(memory_space=pl.ANY), vmem, vmem],
        out_specs=vmem,
        scratch_shapes=[
            pltpu.VMEM((4, ENTRIES, D), I32),
            pltpu.VMEM((3, 8, D), I32),
            pltpu.SMEM((4, ENTRIES, D), I32),
            pltpu.VMEM((POOL, D, D), BF16),
            pltpu.VMEM((POOL, D, D), BF16),
            pltpu.VMEM((8, HALF, D), BF16),
            pltpu.VMEM((2, D, D), F32),
            pltpu.VMEM((NG + 1, D + EXTRA, HALF), F32),
            pltpu.VMEM((NG + 1, 8, HALF), F32),
            pltpu.VMEM((2, WIDE * D, HALF), F32),
            pltpu.VMEM((8, D, HALF), BF16),
            pltpu.VMEM((8, 2, HALF), F32),
            pltpu.VMEM((4, 2, D, HALF), BF16),
            pltpu.VMEM((4, 2, 2, HALF), F32),
            dma((COPIES,)), dma((COPIES,)), dma((2,)), dma(()), dma((8 * HALF // D,)),
            dma((8, 2)), dma((4, 2, 2)), dma((2,)),
        ],
        compiler_params=pltpu.CompilerParams(
            collective_id=0, has_side_effects=True, vmem_limit_bytes=VMEM_LIMIT,
        ),
        name="attend_all",
    )(q_order, block_mask, queries, keys, values)


def on_device(queries, keys, values, q_order, block_mask):
    return fused(q_order, block_mask, queries, keys.reshape(D, 2 * D), values.reshape(D, 2 * D))


def solution(mesh):
    in_specs = (P("pb", "ha"), P("pb", "ka", None, "ha"), P("pb", "ka", None, "ha"), P("pb"), P("pb", None))
    return jax.shard_map(
        on_device, mesh=mesh, in_specs=in_specs, out_specs=P(("pb", "ka"), "ha"), check_vma=False
    )
```
